256 devices in a mesh: inp: 2 (over y_hi), pa: 16 (over x, y_lo, core), pb: 8 (over z).
Axes of the slice: x: 4, y: 4 (y_hi: 2, y_lo: 2; y = y_hi * 2 + y_lo), z: 8, core: 2. Of those that a mesh axis runs over, the one named last changes fastest.
Arguments:
- log_inputs: float32 [2, 256, 256, 256], P('inp', 'pa', 'pb'), may hold values from -6 to 6
- warm_potential: float32 [2, 256, 256, 256], P('inp', 'pa', 'pb'), may hold values from -6 to 6
- bary_weights: float32 [2], P('inp'), may hold values from 0.1 to 0.5
- band_reach: int32 [3], replicated, may hold values from 0 to 2, each once
- bary_cotangent: float32 [256, 256, 256], P('pa', 'pb', 'inp'), may hold values from -6 to 6
Outputs:
- barycenter: float32 [256, 256, 256], P('pa', 'pb', 'inp')
- input_grad: float32 [2, 256, 256, 256], P('inp', 'pa', 'pb')
The draws below stay inside these ranges and needn't reach their ends.
Inputs may be any that keep to these rules, and one draw needn't show every extreme that they name: `band_reach`: a permutation of 0, 1 and 2, one entry a line direction.
All inputs are finite; a program needn't handle non-finite values.
Results may differ from the reference program's by a relative error of at most 0.00022.
Values sent between devices are 32-bit elements; how exact they have to be, the bound alone decides.
A program may use at most 64 MiB of HBM per device.

```python
import math
import jax
import jax.numpy as jnp
from jax import lax

N = 256
K = 2


def block_scale(stream_key, shape, split, low, top_value):
    gain = 1.0
    for dim, blocks in split:
        steps = jax.random.uniform(jax.random.fold_in(jax.random.fold_in(stream_key, 6), dim), (blocks,), jnp.float32, low / len(split), top_value / len(split))
        gain = gain * jnp.repeat(jnp.exp(steps), shape[dim] // blocks).reshape((-1,) + (1,) * (len(shape) - 1 - dim))
    return gain


def centred(rng, dims, spread, bound, cuts=(), kind=jnp.bfloat16):
    gain = block_scale(rng, dims, cuts, -0.22, 0.18) if cuts else 1.0
    result = jax.random.normal(rng, dims, jnp.float32) * spread * gain
    return jnp.minimum(jnp.maximum(result, -bound), bound).astype(kind)


def setup_inputs(seed: int = 0) -> dict:
    splits = jax.random.split(jax.random.key(seed), 6)
    log_inputs = centred(splits[0], (K, N, N, N), 1.0, 6.0, ((0, 2), (1, 16), (2, 8)), jnp.float32)
    warm_potential = centred(splits[1], (K, N, N, N), 1.0, 6.0, ((0, 2), (1, 16), (2, 8)), jnp.float32)
    bary_weights = jnp.clip(jnp.exp(math.log(0.5) - 1.609438 * jax.random.uniform(splits[2], (K,), jnp.float32) ** block_scale(splits[2], (K,), ((0, 2),), -0.2, 0.2)), 0.1, 0.5)
    band_reach = jax.random.permutation(splits[3], 3).astype(jnp.int32)
    bary_cotangent = centred(splits[4], (N, N, N), 1.0, 6.0, ((0, 16), (1, 8), (2, 2)), jnp.float32)
    return dict(log_inputs=log_inputs, warm_potential=warm_potential, bary_weights=bary_weights, band_reach=band_reach, bary_cotangent=bary_cotangent)


FORMS = ('ij,jbc->ibc', 'ij,ajc->aic', 'ij,abj->abi')

def line_kernel(length, reach):
    index = jnp.arange(length, dtype=jnp.int32)
    block = 4
    sigma = 3.0
    offset = (index[:, None] - index[None, :]).astype(jnp.float32)
    inside = jnp.abs(index[:, None] // block - index[None, :] // block) <= reach
    gauss = jnp.exp(-offset * offset / (2.0 * sigma * sigma)) / (sigma * math.sqrt(2.0 * math.pi))
    return 0.5 * jnp.eye(length, dtype=jnp.float32) + 0.5 * jnp.where(inside, gauss, jnp.zeros_like(gauss))

def reference(log_inputs, warm_potential, bary_weights, band_reach, bary_cotangent):
    length = log_inputs.shape[1]
    kernels = [line_kernel(length, band_reach[line]) for line in range(3)]

    def convolve(field):
        for line in range(3):
            field = jnp.log(jnp.einsum(FORMS[line], kernels[line], jnp.exp(field), precision=lax.Precision.HIGHEST))
        return field

    def conv_all(fields):
        return lax.map(convolve, fields)

    def adjoint(pair):
        value, cotan = pair
        unused, pull = jax.vjp(convolve, value)
        return pull(cotan)[0]
    weights = bary_weights[:, None, None, None]
    dual_one = log_inputs - conv_all(warm_potential)
    part_one = warm_potential + conv_all(dual_one)
    barycenter = lax.optimization_barrier(jnp.sum(weights * part_one, axis=0))
    one_bar = weights * bary_cotangent[None]
    input_grad = lax.map(adjoint, (dual_one, one_bar))
    return (barycenter, input_grad)
```

```python
import functools
import math

import jax
import jax.numpy as jnp
from jax import lax
from jax.experimental import pallas as pl
from jax.experimental.pallas import tpu as pltpu
from jax.sharding import PartitionSpec as P

MESH = pl.DeviceIdType.MESH
F32 = jnp.float32
BF16 = jnp.bfloat16
BLOCK = 4
SIGMA = 3.0
TILE = 8
ORDER = (1, 2, 0, 3)


def weight(row, column, reach):
    offset = (row - column).astype(F32)
    inside = jnp.abs(row // BLOCK - column // BLOCK) <= reach
    gauss = jnp.exp(-offset * offset / (2.0 * SIGMA * SIGMA)) / (SIGMA * math.sqrt(2.0 * math.pi))
    return 0.5 * jnp.where(row == column, 1.0, 0.0) + 0.5 * jnp.where(inside, gauss, 0.0)


def iotas(rows, columns):
    shape = (rows, columns)
    return lax.broadcasted_iota(jnp.int32, shape, 0), lax.broadcasted_iota(jnp.int32, shape, 1)


def split(value):
    high = value.astype(BF16)
    return high, (value - high.astype(F32)).astype(BF16)


def dot(a, b):
    return jnp.dot(a, b, preferred_element_type=F32)


def kernel(
    rx, ry, reach_ref, w_ref, warm_hbm, log_hbm, cot_hbm, bary_hbm, grad_hbm,
    warm_v, log_v, u, v, cot_v, part_v, peer_v, bary_v, grad_v,
    mxh, mxl, myh, myl, kzh, kzl,
    in_sem, out_sem, x_send, x_recv, y_send, y_recv, i_send, i_recv,
):
    hx = BLOCK * rx
    inp, pa, pb = (lax.axis_index(name) for name in ("inp", "pa", "pb"))
    last_a, last_b = lax.axis_size("pa") - 1, lax.axis_size("pb") - 1
    has = {
        ("x", 0): pa > 0, ("x", 1): pa < last_a,
        ("y", 0): pb > 0, ("y", 1): pb < last_b,
    }
    near = {
        ("x", 0): {"pa": pa - 1}, ("x", 1): {"pa": pa + 1},
        ("y", 0): {"pb": pb - 1}, ("y", 1): {"pb": pb + 1},
    }
    partner = {"inp": 1 - inp}

    loads = [
        pltpu.make_async_copy(warm_hbm, warm_v, in_sem.at[0]),
        pltpu.make_async_copy(log_hbm, log_v, in_sem.at[1]),
        pltpu.make_async_copy(cot_hbm, cot_v.at[inp], in_sem.at[2]),
    ]
    for load in loads:
        load.start()

    barrier = pltpu.get_barrier_semaphore()
    pl.semaphore_signal(barrier, inc=1, device_id=partner, device_id_type=MESH)
    for key, there in has.items():
        @pl.when(there)
        def _(key=key):
            pl.semaphore_signal(barrier, inc=1, device_id=near[key], device_id_type=MESH)

    row, column = iotas(*mxh.shape)
    entries = weight(row // TILE + hx, column // TILE, reach_ref[0])
    mxh[...], mxl[...] = split(jnp.where(row % TILE == column % TILE, entries, 0.0))
    row, column = iotas(*myh.shape)
    lead = TILE if ry else 0
    entries = weight(row % TILE + lead, (column // 64) * TILE + column % TILE, reach_ref[1])
    mine = row // TILE == (column % 64) // TILE
    myh[...], myl[...] = split(jnp.where(mine, entries, 0.0))
    row, column = iotas(*kzh.shape)
    kzh[...], kzl[...] = split(weight(row, column, reach_ref[2]))

    if rx:
        for side, rows in ((0, pl.ds(0, hx)), (1, pl.ds(hx + 16, hx))):
            @pl.when(jnp.logical_not(has["x", side]))
            def _(rows=rows):
                for turn in range(3):
                    for g in range(4):
                        u[turn, g, rows] = jnp.zeros((hx, TILE, 256), F32)
    if ry:
        for side, g in ((0, 0), (1, 5)):
            @pl.when(jnp.logical_not(has["y", side]))
            def _(g=g):
                for turn in range(3):
                    v[turn, g] = jnp.zeros((16, TILE, 256), F32)

    own = pl.ds(hx, 16)

    def tile(ref, g):
        return ref[:, pl.ds(TILE * g, TILE), :]

    loads[0].wait()
    for g in ORDER:
        u[0, g, own] = jnp.exp(tile(warm_v, g))

    pl.semaphore_wait(barrier, 1 + sum(there.astype(jnp.int32) for there in has.values()))

    def x_copy(turn, g, side):
        source = u.at[turn, g, pl.ds(hx + (0 if side == 0 else 16 - hx), hx)]
        target = u.at[turn, g, pl.ds(hx + 16 if side == 0 else 0, hx)]
        return pltpu.make_async_remote_copy(
            src_ref=source, dst_ref=target,
            send_sem=x_send.at[turn, g, side], recv_sem=x_recv.at[turn, g, 1 - side],
            device_id=near["x", side], device_id_type=MESH,
        )

    def x_arrival(turn, g, side):
        target = u.at[turn, g, pl.ds(0 if side == 0 else hx + 16, hx)]
        return pltpu.make_async_remote_copy(
            src_ref=target, dst_ref=target,
            send_sem=x_send.at[turn, g, side], recv_sem=x_recv.at[turn, g, side],
            device_id=near["x", side], device_id_type=MESH,
        )

    def y_copy(turn, side):
        return pltpu.make_async_remote_copy(
            src_ref=v.at[turn, 1 if side == 0 else 4], dst_ref=v.at[turn, 5 if side == 0 else 0],
            send_sem=y_send.at[turn, side], recv_sem=y_recv.at[turn, 1 - side],
            device_id=near["y", side], device_id_type=MESH,
        )

    def y_arrival(turn, side):
        target = v.at[turn, 0 if side == 0 else 5]
        return pltpu.make_async_remote_copy(
            src_ref=target, dst_ref=target,
            send_sem=y_send.at[turn, side], recv_sem=y_recv.at[turn, side],
            device_id=near["y", side], device_id_type=MESH,
        )

    def peer_copy(which, source, target):
        return pltpu.make_async_remote_copy(
            src_ref=source, dst_ref=target, send_sem=i_send.at[which], recv_sem=i_recv.at[which],
            device_id=partner, device_id_type=MESH,
        )

    def x_start(turn, g):
        if rx:
            for side in (0, 1):
                @pl.when(has["x", side])
                def _(side=side):
                    x_copy(turn, g, side).start()

    def x_wait(turn, g):
        if rx:
            for side in (0, 1):
                @pl.when(has["x", side])
                def _(side=side):
                    x_arrival(turn, g, side).wait_recv()

    def y_start(turn, side):
        if ry:
            @pl.when(has["y", side])
            def _():
                y_copy(turn, side).start()

    def y_wait(turn, side):
        if ry:
            @pl.when(has["y", side])
            def _():
                y_arrival(turn, side).wait_recv()

    for g in ORDER:
        x_start(0, g)
    loads[2].wait()
    cot_copy = peer_copy(0, cot_v.at[inp], cot_v.at[inp])
    cot_copy.start()
    loads[1].wait()

    lead_y = 1 if ry else 0
    depth_y = 3 if ry else 1
    stores = []
    for turn in range(3):
        for g in ORDER:
            x_wait(turn, g)
            high, low = split(u[turn, g].reshape(-1, 256))
            done = dot(mxh[...], high) + dot(mxl[...], high) + dot(mxh[...], low)
            v[turn, g + lead_y] = done.reshape(16, TILE, 256)
            if g == 0:
                y_start(turn, 0)
            if g == 3:
                y_start(turn, 1)
        if turn == 1:
            peer_copy(0, cot_v.at[1 - inp], cot_v.at[1 - inp]).wait_recv()
        for g in ORDER:
            if g == 0:
                y_wait(turn, 0)
            if g == 3:
                y_wait(turn, 1)
            halves = []
            for half in (0, 1):
                piece = v[turn, pl.ds(g, depth_y), pl.ds(8 * half, 8)].reshape(-1, 256)
                high, low = split(piece)
                halves.append(dot(myh[...], high) + dot(myl[...], high) + dot(myh[...], low))
            high, low = split(jnp.concatenate(halves, axis=0))
            done = dot(high, kzh[...]) + dot(low, kzh[...]) + dot(high, kzl[...])
            done = done.reshape(16, TILE, 256)
            if turn == 0:
                u[1, g, own] = jnp.exp(tile(log_v, g)) / done
                x_start(1, g)
            elif turn == 1:
                part = w_ref[0] * (tile(warm_v, g) + jnp.log(done))
                part_v[0, :, pl.ds(TILE * g, TILE), :] = part[:, :, :128]
                part_v[1, :, pl.ds(TILE * g, TILE), :] = part[:, :, 128:]
                cot = jnp.concatenate(
                    [cot_v[0, :, pl.ds(TILE * g, TILE), :], cot_v[1, :, pl.ds(TILE * g, TILE), :]], axis=2
                )
                u[2, g, own] = (w_ref[0] * cot) / done
                x_start(2, g)
            else:
                grad_v[:, pl.ds(TILE * g, TILE), :] = u[1, g, own] * done
        if turn == 1:
            part_copy = peer_copy(1, part_v.at[1 - inp], peer_v)
            part_copy.start()

    store = pltpu.make_async_copy(grad_v, grad_hbm, out_sem.at[0])
    store.start()
    stores.append(store)
    part_copy.wait_recv()
    bary_v[...] = part_v[inp] + peer_v[...]
    store = pltpu.make_async_copy(bary_v, bary_hbm, out_sem.at[1])
    store.start()
    stores.append(store)

    cot_copy.wait_send()
    part_copy.wait_send()
    for turn in range(3):
        for side in (0, 1):
            if rx:
                @pl.when(has["x", side])
                def _(turn=turn, side=side):
                    for g in range(4):
                        x_copy(turn, g, side).wait_send()
            if ry:
                @pl.when(has["y", side])
                def _(turn=turn, side=side):
                    y_copy(turn, side).wait_send()
    for store in stores:
        store.wait()


def fused(rx, ry, band_reach, weights, warm, log_inputs, cotangent):
    hx = BLOCK * rx
    depth_y = 3 if ry else 1
    groups_y = 6 if ry else 4
    any_space = pl.BlockSpec(memory_space=pl.ANY)
    smem = pl.BlockSpec(memory_space=pltpu.SMEM)
    dma = pltpu.SemaphoreType.DMA
    field = pltpu.VMEM((16, 32, 256), F32)
    half = pltpu.VMEM((16, 32, 128), F32)
    matrix_x = pltpu.VMEM((128, 8 * (16 + 2 * hx)), BF16)
    matrix_y = pltpu.VMEM((64, 64 * depth_y), BF16)
    matrix_z = pltpu.VMEM((256, 256), BF16)
    return pl.pallas_call(
        functools.partial(kernel, rx, ry),
        out_shape=(
            jax.ShapeDtypeStruct((16, 32, 128), F32),
            jax.ShapeDtypeStruct((16, 32, 256), F32),
        ),
        in_specs=[smem, smem, any_space, any_space, any_space],
        out_specs=(any_space, any_space),
        scratch_shapes=[
            field, field,
            pltpu.VMEM((3, 4, 16 + 2 * hx, TILE, 256), F32),
            pltpu.VMEM((3, groups_y, 16, TILE, 256), F32),
            pltpu.VMEM((2, 16, 32, 128), F32),
            pltpu.VMEM((2, 16, 32, 128), F32),
            half, half, field,
            matrix_x, matrix_x, matrix_y, matrix_y, matrix_z, matrix_z,
            dma((3,)), dma((2,)),
            dma((3, 4, 2)), dma((3, 4, 2)), dma((3, 2)), dma((3, 2)), dma((2,)), dma((2,)),
        ],
        compiler_params=pltpu.CompilerParams(
            collective_id=3 * rx + ry, has_side_effects=True, vmem_limit_bytes=40 << 20
        ),
    )(band_reach, weights, warm, log_inputs, cotangent)


def per_device(log_inputs, warm_potential, bary_weights, band_reach, bary_cotangent):
    barycenter, input_grad = fused(
        2, 2, band_reach, bary_weights, warm_potential[0], log_inputs[0], bary_cotangent
    )
    return barycenter, input_grad[None]


def solution(mesh):
    return jax.shard_map(
        per_device,
        mesh=mesh,
        in_specs=(
            P("inp", "pa", "pb", None),
            P("inp", "pa", "pb", None),
            P("inp"),
            P(),
            P("pa", "pb", "inp"),
        ),
        out_specs=(P("pa", "pb", "inp"), P("inp", "pa", "pb", None)),
        check_vma=False,
    )
```

```python
import functools
import math

import jax
import jax.numpy as jnp
from jax import lax
from jax.experimental import pallas as pl
from jax.experimental.pallas import tpu as pltpu
from jax.sharding import PartitionSpec as P

MESH = pl.DeviceIdType.MESH
F32 = jnp.float32
BF16 = jnp.bfloat16
BLOCK = 4
SIGMA = 3.0
OUTER, INNER = (0, 3), (1, 2)
CASES = ((0, 1), (0, 2), (1, 0), (1, 2), (2, 0), (2, 1))


def weight(row, column, reach):
    offset = (row - column).astype(F32)
    inside = jnp.abs(row // BLOCK - column // BLOCK) <= reach
    gauss = jnp.exp(-offset * offset / (2.0 * SIGMA * SIGMA)) / (SIGMA * math.sqrt(2.0 * math.pi))
    return 0.5 * jnp.where(row == column, 1.0, 0.0) + 0.5 * jnp.where(inside, gauss, 0.0)


def iotas(rows, columns):
    shape = (rows, columns)
    return lax.broadcasted_iota(jnp.int32, shape, 0), lax.broadcasted_iota(jnp.int32, shape, 1)


def split(value):
    high = value.astype(BF16)
    return high, (value - high.astype(F32)).astype(BF16)


def stacked(value):
    return jnp.concatenate(split(value), axis=0)


def doubled(matrix):
    high, low = split(matrix)
    return jnp.concatenate(
        [jnp.concatenate([high, high], axis=1), jnp.concatenate([low, low], axis=1)], axis=0
    )


def dot(a, b):
    return jnp.dot(a, b, preferred_element_type=F32)


def product(left, parts):
    both = dot(left, parts)
    rows = both.shape[0] // 2
    return both[:rows] + both[rows:]


def kernel(
    rx, ry, w_ref, warm_hbm, log_hbm, cot_hbm, bary_v, grad_v,
    warm_v, log_v, cot_v, own, x_halo, y_out, y_halo, acc_x, acc_y, v_high, v_low,
    part_v, peer_v, mx, mxh, my, myh, kzh, kzl,
    in_sem, x_send, x_recv, y_send, y_recv, i_send, i_recv,
):
    rz = 3 - rx - ry
    hx = BLOCK * rx
    inp, pa, pb = (lax.axis_index(name) for name in ("inp", "pa", "pb"))
    near_x = ({"pa": pa - 1}, {"pa": pa + 1})
    near_y = ({"pb": pb - 1}, {"pb": pb + 1})
    has_x = (pa > 0, pa < lax.axis_size("pa") - 1)
    has_y = (pb > 0, pb < lax.axis_size("pb") - 1)
    partner = {"inp": 1 - inp}

    loads = [
        pltpu.make_async_copy(warm_hbm, warm_v, in_sem.at[0]),
        pltpu.make_async_copy(cot_hbm, cot_v.at[inp], in_sem.at[1]),
        pltpu.make_async_copy(log_hbm, log_v, in_sem.at[2]),
    ]
    for load in loads:
        load.start()

    barrier = pltpu.get_barrier_semaphore()
    pl.semaphore_signal(barrier, inc=1, device_id=partner, device_id_type=MESH)
    others = 1
    for near, has, used in ((near_x, has_x, rx), (near_y, has_y, ry)):
        for side in (0, 1):
            if used:
                @pl.when(has[side])
                def _(device=near[side]):
                    pl.semaphore_signal(barrier, inc=1, device_id=device, device_id_type=MESH)
                others = others + has[side].astype(jnp.int32)

    for side in (0, 1):
        if rx:
            @pl.when(jnp.logical_not(has_x[side]))
            def _(side=side):
                x_halo[:, :, side] = jnp.zeros((3, 4, hx, 8, 256), F32)
        if ry:
            @pl.when(jnp.logical_not(has_y[side]))
            def _(side=side):
                y_halo[:, side] = jnp.zeros((3, *y_halo.shape[2:]), F32)

    if rx:
        row, column = iotas(128, 128)
        lines = weight(row % 8, column % 8, 0) if ry == 0 else (row % 8 == column % 8).astype(F32)
        mx[...] = doubled(lines * weight(row // 8, column // 8, rx))
        row, column = iotas(128, 16 * hx)
        place = jnp.where(column < 8 * hx, column // 8, 16 + column // 8)
        lines = weight(row % 8, column % 8, 0) if ry == 0 else (row % 8 == column % 8).astype(F32)
        mxh[...] = doubled(lines * weight(row // 8 + hx, place, rx))
    if ry:
        def lines_x(row, column):
            return (row == column).astype(F32) if rx else weight(row, column, 0)

        row, column = iotas(128, 128)
        entries = weight(8 * (row // 32) + row % 8, 8 * (column // 32) + column % 8, ry)
        my[...] = doubled(lines_x((row % 32) // 8, (column % 32) // 8) * entries)
    if ry == 2:
        place = jnp.where(column < 64, column % 8, 40 + column % 8)
        entries = weight(8 + 24 * (row // 64) + row % 8, place, ry)
        myh[...] = doubled(lines_x((row % 64) // 8, (column % 64) // 8) * entries)
    if ry == 1:
        row, column = iotas(256, 128)
        place = jnp.where(column < 64, column % 4, 36 + column % 4)
        entries = weight(4 + 24 * (row // 128) + row % 8, place, ry)
        line = 2 * ((column % 64) // 8) + (column % 8) // 4
        myh[...] = doubled(lines_x((row % 128) // 8, line) * entries)
    row, column = iotas(256, 256)
    kzh[...], kzl[...] = split(weight(row, column, rz))

    def tile(ref, g):
        return ref[:, pl.ds(8 * g, 8), :]

    def remote(source, target, send, recv, device):
        return pltpu.make_async_remote_copy(
            src_ref=source, dst_ref=target, send_sem=send, recv_sem=recv,
            device_id=device, device_id_type=MESH,
        )

    def x_copy(turn, g, side):
        return remote(
            own.at[turn, g, pl.ds(0 if side == 0 else 16 - hx, hx)], x_halo.at[turn, g, 1 - side],
            x_send.at[turn, g, side], x_recv.at[turn, g, 1 - side], near_x[side],
        )

    def y_copy(turn, side):
        whole = ry == 2 and rx == 0
        return remote(
            own.at[turn, OUTER[side]] if whole else y_out.at[turn, side], y_halo.at[turn, 1 - side],
            y_send.at[turn, side], y_recv.at[turn, 1 - side], near_y[side],
        )

    def cot_copy(piece, slot):
        rows = pl.ds(8 * piece, 8)
        return remote(
            cot_v.at[slot, rows], cot_v.at[slot, rows], i_send.at[piece], i_recv.at[piece], partner
        )

    def part_copy(g):
        return remote(
            part_v.at[1 - inp, g], peer_v.at[g], i_send.at[2 + g], i_recv.at[2 + g], partner
        )

    def x_start(turn, pair):
        for side in (0, 1):
            @pl.when(has_x[side])
            def _(side=side):
                for g in pair:
                    x_copy(turn, g, side).start()

    def y_start(turn, g, value):
        side = OUTER.index(g)
        if ry == 2 and rx:
            y_out[turn, side] = value
        if ry == 1:
            value = value.reshape(8, 2, 8, 256)
            start = 4 * side
            y_out[turn, side] = jnp.concatenate(
                [value[:, 0, start : start + 4], value[:, 1, start : start + 4]], axis=1
            )

        @pl.when(has_y[side])
        def _():
            y_copy(turn, side).start()

    def enter(turn, pair):
        if rx:
            x_start(turn, pair)
        else:
            for g in pair:
                if g in OUTER:
                    y_start(turn, g, own[turn, g])

    def own_part(turn, pair):
        for g in pair:
            value = own[turn, g].reshape(128, 256)
            if rx:
                acc_x[g] = product(mx[...], stacked(value))
            else:
                v_high[g], v_low[g] = split(value)

    def x_finish(turn, pair):
        for side in (0, 1):
            @pl.when(has_x[side])
            def _(side=side):
                for g in pair:
                    x_copy(turn, g, 1 - side).wait_recv()
        totals = []
        for g in pair:
            halo = x_halo[turn, g].reshape(16 * hx, 256)
            totals.append(acc_x[g] + product(mxh[...], stacked(halo)))
        return totals

    def y_own():
        for q in range(4):
            rows = pl.ds(32 * q, 32)
            parts = jnp.concatenate(
                [v_high[:, rows].reshape(128, 256), v_low[:, rows].reshape(128, 256)], axis=0
            )
            acc_y[:, rows] = product(my[...], parts).reshape(4, 32, 256)

    def y_finish(turn):
        for side in (0, 1):
            @pl.when(has_y[side])
            def _(side=side):
                y_copy(turn, 1 - side).wait_recv()
        if ry == 2:
            pieces = []
            for half in (0, 1):
                halo = y_halo[turn, :, pl.ds(8 * half, 8)].reshape(128, 256)
                pieces.append(product(myh[...], stacked(halo)))
            more = [jnp.concatenate([p[64 * e : 64 * e + 64] for p in pieces], axis=0) for e in (0, 1)]
        else:
            both = product(myh[...], stacked(y_halo[turn].reshape(128, 256)))
            more = [both[:128], both[128:]]
        return [acc_y[g] + extra for g, extra in zip(OUTER, more)]

    def epilogue(turn, pair, totals):
        high, low = split(jnp.concatenate(totals, axis=0))
        both = dot(jnp.concatenate([high, low], axis=0), kzh[...])
        both = both[:256] + both[256:] + dot(high, kzl[...])
        done = [both[:128].reshape(16, 8, 256), both[128:].reshape(16, 8, 256)]
        for g, value in zip(pair, done):
            if turn == 0:
                own[1, g] = jnp.exp(tile(log_v, g)) / value
            elif turn == 1:
                cot = jnp.concatenate([tile(cot_v.at[0], g), tile(cot_v.at[1], g)], axis=2)
                own[2, g] = (w_ref[0] * cot) / value
            else:
                grad_v[:, pl.ds(8 * g, 8), :] = own[1, g] * value
        if turn == 2:
            return
        enter(turn + 1, pair)
        if turn == 1:
            for g, value in zip(pair, done):
                part = w_ref[0] * (tile(warm_v, g) + jnp.log(value))
                part_v[0, g] = part[:, :, :128]
                part_v[1, g] = part[:, :, 128:]
        own_part(turn + 1, pair)

    loads[0].wait()
    for g in OUTER + INNER:
        own[0, g] = jnp.exp(tile(warm_v, g))
    loads[1].wait()
    pl.semaphore_wait(barrier, others)

    first, second = (OUTER, INNER) if rx == 2 or ry == 0 else (INNER, OUTER)

    enter(0, OUTER)
    if rx:
        enter(0, INNER)
    cot_copy(0, inp).start()
    if rx < 2:
        cot_copy(1, inp).start()
    own_part(0, OUTER)
    own_part(0, INNER)
    loads[2].wait()

    for turn in range(3):
        if rx and ry:
            for pair in (OUTER, INNER) if turn == 0 else (first, second):
                for g, total in zip(pair, x_finish(turn, pair)):
                    v_high[g], v_low[g] = split(total)
                    if g in OUTER:
                        y_start(turn, g, total.reshape(16, 8, 256))
        if ry:
            y_own()
        if turn == 1:
            for piece in (0, 1):
                cot_copy(piece, 1 - inp).wait_recv()
        for pair in (first, second):
            if ry == 0:
                totals = x_finish(turn, pair)
            elif pair == OUTER:
                totals = y_finish(turn)
            else:
                totals = [acc_y[g] for g in pair]
            epilogue(turn, pair, totals)
            if turn == 1 and rx == 0:
                for g in pair:
                    part_copy(g).start()
        if turn == 0 and rx == 2:
            cot_copy(1, inp).start()
        if turn == 1 and rx:
            for g in first + second:
                part_copy(g).start()

    for g in first + second:
        part_copy(g).wait_recv()
        bary_v[:, pl.ds(8 * g, 8), :] = part_v[inp, g] + peer_v[g]

    for piece in (0, 1):
        cot_copy(piece, inp).wait_send()
    for g in range(4):
        part_copy(g).wait_send()
    for side in (0, 1):
        if rx:
            @pl.when(has_x[side])
            def _(side=side):
                for turn in range(3):
                    for g in range(4):
                        x_copy(turn, g, side).wait_send()
        if ry:
            @pl.when(has_y[side])
            def _(side=side):
                for turn in range(3):
                    y_copy(turn, side).wait_send()


def fused(rx, ry, weights, warm, log_inputs, cotangent):
    hx = BLOCK * rx
    hbm = pl.BlockSpec(memory_space=pltpu.HBM)
    smem = pl.BlockSpec(memory_space=pltpu.SMEM)
    vmem = pl.BlockSpec(memory_space=pltpu.VMEM)
    dma = pltpu.SemaphoreType.DMA
    field = pltpu.VMEM((16, 32, 256), F32)
    halves = pltpu.VMEM((2, 16, 32, 128), F32)
    rows_y = 16 if ry == 2 else 8
    matrix = pltpu.VMEM((256, 256), BF16)
    return pl.pallas_call(
        functools.partial(kernel, rx, ry),
        out_shape=(
            jax.ShapeDtypeStruct((16, 32, 128), F32),
            jax.ShapeDtypeStruct((16, 32, 256), F32),
        ),
        in_specs=[smem, hbm, hbm, hbm],
        out_specs=(vmem, vmem),
        scratch_shapes=[
            field, field, halves,
            pltpu.VMEM((3, 4, 16, 8, 256), F32),
            pltpu.VMEM((3, 4, 2, max(hx, 1), 8, 256), F32),
            pltpu.VMEM((3, 2, rows_y, 8, 256), F32),
            pltpu.VMEM((3, 2, rows_y, 8, 256), F32),
            pltpu.VMEM((4, 128, 256), F32),
            pltpu.VMEM((4, 128, 256), F32),
            pltpu.VMEM((4, 128, 256), BF16),
            pltpu.VMEM((4, 128, 256), BF16),
            pltpu.VMEM((2, 4, 16, 8, 128), F32),
            pltpu.VMEM((4, 16, 8, 128), F32),
            matrix,
            pltpu.VMEM((256, 32 * max(hx, 4)), BF16),
            matrix,
            pltpu.VMEM((512 if ry == 1 else 256, 256), BF16),
            matrix, matrix,
            dma((3,)), dma((3, 4, 2)), dma((3, 4, 2)), dma((3, 2)), dma((3, 2)), dma((6,)), dma((6,)),
        ],
        compiler_params=pltpu.CompilerParams(
            collective_id=3 * rx + ry, has_side_effects=True, vmem_limit_bytes=40 << 20
        ),
    )(weights, warm, log_inputs, cotangent)


def store(bary_v, grad_v, bary_hbm, grad_hbm, sems):
    copies = [
        pltpu.make_async_copy(bary_v, bary_hbm, sems.at[0]),
        pltpu.make_async_copy(grad_v, grad_hbm, sems.at[1]),
    ]
    for copy in copies:
        copy.start()
    for copy in copies:
        copy.wait()


def stored(bary, grad):
    vmem = pl.BlockSpec(memory_space=pltpu.VMEM)
    hbm = pl.BlockSpec(memory_space=pltpu.HBM)
    return pl.pallas_call(
        store,
        out_shape=(
            jax.ShapeDtypeStruct(bary.shape, F32),
            jax.ShapeDtypeStruct(grad.shape, F32),
        ),
        in_specs=[vmem, vmem],
        out_specs=(hbm, hbm),
        scratch_shapes=[pltpu.SemaphoreType.DMA((2,))],
    )(bary, grad)


def choose(reach_ref, index_ref):
    index_ref[0] = 2 * reach_ref[0] + (reach_ref[1] > reach_ref[2]).astype(jnp.int32)


def per_device(log_inputs, warm_potential, bary_weights, band_reach, bary_cotangent):
    index = pl.pallas_call(
        choose,
        out_shape=jax.ShapeDtypeStruct((1,), jnp.int32),
        in_specs=[pl.BlockSpec(memory_space=pltpu.SMEM)],
        out_specs=pl.BlockSpec(memory_space=pltpu.SMEM),
    )(band_reach)[0]
    branches = [functools.partial(fused, rx, ry) for rx, ry in CASES]
    bary, grad = lax.switch(
        index, branches, bary_weights, warm_potential[0], log_inputs[0], bary_cotangent
    )
    bary, grad = stored(bary, grad)
    return bary, grad[None]


def solution(mesh):
    return jax.shard_map(
        per_device,
        mesh=mesh,
        in_specs=(
            P("inp", "pa", "pb", None),
            P("inp", "pa", "pb", None),
            P("inp"),
            P(),
            P("pa", "pb", "inp"),
        ),
        out_specs=(P("pa", "pb", "inp"), P("inp", "pa", "pb", None)),
        check_vma=False,
    )
```

```python
import functools
import math

import jax
import jax.numpy as jnp
from jax import lax
from jax.experimental import pallas as pl
from jax.experimental.pallas import tpu as pltpu
from jax.sharding import PartitionSpec as P

MESH = pl.DeviceIdType.MESH
F32 = jnp.float32
BF16 = jnp.bfloat16
BLOCK = 4
SIGMA = 3.0
OUTER, INNER = (0, 3), (1, 2)
LOG = 4
CASES = ((0, 1), (0, 2), (1, 0), (1, 2), (2, 0), (2, 1))


def weight(row, column, reach):
    offset = (row - column).astype(F32)
    inside = jnp.abs(row // BLOCK - column // BLOCK) <= reach
    gauss = jnp.exp(-offset * offset / (2.0 * SIGMA * SIGMA)) / (SIGMA * math.sqrt(2.0 * math.pi))
    return 0.5 * jnp.where(row == column, 1.0, 0.0) + 0.5 * jnp.where(inside, gauss, 0.0)


def iotas(rows, columns):
    shape = (rows, columns)
    return lax.broadcasted_iota(jnp.int32, shape, 0), lax.broadcasted_iota(jnp.int32, shape, 1)


def split(value):
    high = value.astype(BF16)
    return high, (value - high.astype(F32)).astype(BF16)


def stacked(value):
    return jnp.concatenate(split(value), axis=0)


def doubled(matrix):
    high, low = split(matrix)
    return jnp.concatenate(
        [jnp.concatenate([high, high], axis=1), jnp.concatenate([low, low], axis=1)], axis=0
    )


def dot(a, b):
    return jnp.dot(a, b, preferred_element_type=F32)


def product(left, parts):
    both = dot(left, parts)
    rows = both.shape[0] // 2
    return both[:rows] + both[rows:]


def kernel(
    rx, ry, w_ref, warm_hbm, log_hbm, cot_hbm, bary_v, grad_v,
    warm_v, log_v, cot_v, own, image, x_halo, y_out, y_halo, acc_x, acc_y, v_high, v_low,
    part_v, peer_v, mx, mxh, my, myh, kzh, kzl,
    in_sem, x_send, x_recv, y_send, y_recv, i_send, i_recv,
):
    rz = 3 - rx - ry
    hx = BLOCK * rx
    inp, pa, pb = (lax.axis_index(name) for name in ("inp", "pa", "pb"))
    near_x = ({"pa": pa - 1}, {"pa": pa + 1})
    near_y = ({"pb": pb - 1}, {"pb": pb + 1})
    has_x = (pa > 0, pa < lax.axis_size("pa") - 1)
    has_y = (pb > 0, pb < lax.axis_size("pb") - 1)
    partner = {"inp": 1 - inp}

    loads = [
        pltpu.make_async_copy(warm_hbm, warm_v, in_sem.at[0]),
        pltpu.make_async_copy(cot_hbm, cot_v.at[inp], in_sem.at[1]),
        pltpu.make_async_copy(log_hbm, log_v, in_sem.at[2]),
    ]
    for load in loads:
        load.start()

    barrier = pltpu.get_barrier_semaphore()
    pl.semaphore_signal(barrier, inc=1, device_id=partner, device_id_type=MESH)
    others = 1
    for near, has, used in ((near_x, has_x, rx), (near_y, has_y, ry)):
        for side in (0, 1):
            if used:
                @pl.when(has[side])
                def _(device=near[side]):
                    pl.semaphore_signal(barrier, inc=1, device_id=device, device_id_type=MESH)
                others = others + has[side].astype(jnp.int32)

    for side in (0, 1):
        if rx:
            @pl.when(jnp.logical_not(has_x[side]))
            def _(side=side):
                x_halo[:, :, side] = jnp.zeros((3, 4, hx, 8, 256), F32)
        if ry:
            @pl.when(jnp.logical_not(has_y[side]))
            def _(side=side):
                y_halo[:, side] = jnp.zeros((3, *y_halo.shape[2:]), F32)

    if rx:
        row, column = iotas(128, 128)
        lines = weight(row % 8, column % 8, 0) if ry == 0 else (row % 8 == column % 8).astype(F32)
        mx[...] = doubled(lines * weight(row // 8, column // 8, rx))
        row, column = iotas(128, 16 * hx)
        place = jnp.where(column < 8 * hx, column // 8, 16 + column // 8)
        lines = weight(row % 8, column % 8, 0) if ry == 0 else (row % 8 == column % 8).astype(F32)
        mxh[...] = doubled(lines * weight(row // 8 + hx, place, rx))
    if ry:
        def lines_x(row, column):
            return (row == column).astype(F32) if rx else weight(row, column, 0)

        row, column = iotas(128, 128)
        entries = weight(8 * (row // 32) + row % 8, 8 * (column // 32) + column % 8, ry)
        my[...] = doubled(lines_x((row % 32) // 8, (column % 32) // 8) * entries)
    if ry == 2:
        place = jnp.where(column < 64, column % 8, 40 + column % 8)
        entries = weight(8 + 24 * (row // 64) + row % 8, place, ry)
        myh[...] = doubled(lines_x((row % 64) // 8, (column % 64) // 8) * entries)
    if ry == 1:
        row, column = iotas(256, 128)
        place = jnp.where(column < 64, column % 4, 36 + column % 4)
        entries = weight(4 + 24 * (row // 128) + row % 8, place, ry)
        line = 2 * ((column % 64) // 8) + (column % 8) // 4
        myh[...] = doubled(lines_x((row % 128) // 8, line) * entries)
    row, column = iotas(256, 256)
    kzh[...], kzl[...] = split(weight(row, column, rz))

    def tile(ref, g):
        return ref[:, pl.ds(8 * g, 8), :]

    def remote(source, target, send, recv, device):
        return pltpu.make_async_remote_copy(
            src_ref=source, dst_ref=target, send_sem=send, recv_sem=recv,
            device_id=device, device_id_type=MESH,
        )

    def x_copy(turn, g, side):
        return remote(
            own.at[turn, g, pl.ds(0 if side == 0 else 16 - hx, hx)], x_halo.at[turn, g, 1 - side],
            x_send.at[turn, g, side], x_recv.at[turn, g, 1 - side], near_x[side],
        )

    def y_copy(turn, side):
        whole = ry == 2 and rx == 0
        return remote(
            own.at[turn, OUTER[side]] if whole else y_out.at[turn, side], y_halo.at[turn, 1 - side],
            y_send.at[turn, side], y_recv.at[turn, 1 - side], near_y[side],
        )

    def cot_copy(piece, slot):
        rows = pl.ds(8 * piece, 8)
        return remote(
            cot_v.at[slot, rows], cot_v.at[slot, rows], i_send.at[piece], i_recv.at[piece], partner
        )

    def part_copy(g):
        return remote(
            part_v.at[1 - inp, g], peer_v.at[g], i_send.at[2 + g], i_recv.at[2 + g], partner
        )

    def x_start(turn, pair):
        for side in (0, 1):
            @pl.when(has_x[side])
            def _(side=side):
                for g in pair:
                    x_copy(turn, g, side).start()

    def y_start(turn, g, value):
        side = OUTER.index(g)
        if ry == 2 and rx:
            y_out[turn, side] = value
        if ry == 1:
            value = value.reshape(8, 2, 8, 256)
            start = 4 * side
            y_out[turn, side] = jnp.concatenate(
                [value[:, 0, start : start + 4], value[:, 1, start : start + 4]], axis=1
            )

        @pl.when(has_y[side])
        def _():
            y_copy(turn, side).start()

    def enter(turn, pair):
        if rx:
            x_start(turn, pair)
        else:
            for g in pair:
                if g in OUTER:
                    y_start(turn, g, own[turn, g])

    def own_part(turn, pair):
        for g in pair:
            value = own[turn, g].reshape(128, 256)
            if rx:
                acc_x[g] = product(mx[...], stacked(value))
            else:
                v_high[g], v_low[g] = split(value)

    def x_finish(turn, pair):
        for side in (0, 1):
            @pl.when(has_x[side])
            def _(side=side):
                for g in pair:
                    x_copy(turn, g, 1 - side).wait_recv()
        totals = []
        for g in pair:
            halo = x_halo[turn, g].reshape(16 * hx, 256)
            totals.append(acc_x[g] + product(mxh[...], stacked(halo)))
        return totals

    def y_own():
        for q in range(4):
            rows = pl.ds(32 * q, 32)
            parts = jnp.concatenate(
                [v_high[:, rows].reshape(128, 256), v_low[:, rows].reshape(128, 256)], axis=0
            )
            acc_y[:, rows] = product(my[...], parts).reshape(4, 32, 256)

    def y_finish(turn):
        for side in (0, 1):
            @pl.when(has_y[side])
            def _(side=side):
                y_copy(turn, 1 - side).wait_recv()
        if ry == 2:
            pieces = []
            for half in (0, 1):
                halo = y_halo[turn, :, pl.ds(8 * half, 8)].reshape(128, 256)
                pieces.append(product(myh[...], stacked(halo)))
            more = [jnp.concatenate([p[64 * e : 64 * e + 64] for p in pieces], axis=0) for e in (0, 1)]
        else:
            both = product(myh[...], stacked(y_halo[turn].reshape(128, 256)))
            more = [both[:128], both[128:]]
        return [acc_y[g] + extra for g, extra in zip(OUTER, more)]

    def epilogue(turn, pair, totals):
        high, low = split(jnp.concatenate(totals, axis=0))
        both = dot(jnp.concatenate([high, low], axis=0), kzh[...])
        both = both[:256] + both[256:] + dot(high, kzl[...])
        factor = jnp.where(turn == 2, 1, turn + LOG)
        for g, value in zip(pair, (both[:128], both[128:])):
            value = value.reshape(16, 8, 256)
            image[g] = value
            own[turn + 1, g] = own[factor, g] * jnp.where(turn == 2, value, 1.0 / value)

        @pl.when(turn < 2)
        def _():
            enter(turn + 1, pair)

        @pl.when(turn == 1)
        def _():
            for g in pair:
                part = w_ref[0] * (tile(warm_v, g) + jnp.log(image[g]))
                part_v[0, g] = part[:, :, :128]
                part_v[1, g] = part[:, :, 128:]
            if rx == 0:
                for g in pair:
                    part_copy(g).start()

        @pl.when(turn < 2)
        def _():
            own_part(turn + 1, pair)

    loads[0].wait()
    for g in OUTER + INNER:
        own[0, g] = jnp.exp(tile(warm_v, g))
    loads[1].wait()
    pl.semaphore_wait(barrier, others)

    first, second = (OUTER, INNER) if rx == 2 or ry == 0 else (INNER, OUTER)

    enter(0, OUTER)
    if rx:
        enter(0, INNER)
    else:
        cot_copy(0, inp).start()
        cot_copy(1, inp).start()
    own_part(0, OUTER)
    own_part(0, INNER)
    loads[2].wait()
    for g in range(4):
        own[LOG, g] = jnp.exp(tile(log_v, g))

    def body(turn, carry):
        if rx and ry:
            for pair in (OUTER, INNER):
                for g, total in zip(pair, x_finish(turn, pair)):
                    v_high[g], v_low[g] = split(total)
                    if g in OUTER:
                        y_start(turn, g, total.reshape(16, 8, 256))
                if pair == OUTER:
                    @pl.when(turn == 0)
                    def _():
                        cot_copy(0, inp).start()
        if ry:
            y_own()

        @pl.when(turn == 1)
        def _():
            for piece in (0, 1):
                cot_copy(piece, 1 - inp).wait_recv()
            for g in range(4):
                own[LOG + 1, g, :, :, :128] = w_ref[0] * tile(cot_v.at[0], g)
                own[LOG + 1, g, :, :, 128:] = w_ref[0] * tile(cot_v.at[1], g)

        for pair in (first, second):
            if ry == 0:
                totals = x_finish(turn, pair)
            elif pair == OUTER:
                totals = y_finish(turn)
            else:
                totals = [acc_y[g] for g in pair]
            epilogue(turn, pair, totals)
            if ry == 0:
                @pl.when(turn == 0)
                def _(pair=pair):
                    cot_copy((first, second).index(pair), inp).start()

        if rx:
            @pl.when(turn == 1)
            def _():
                for g in first + second:
                    part_copy(g).start()
        if rx and ry:
            @pl.when(turn == 0)
            def _():
                cot_copy(1, inp).start()
        return carry

    lax.fori_loop(0, 3, body, 0)

    for g in range(4):
        grad_v[:, pl.ds(8 * g, 8), :] = own[3, g]
    for g in first + second:
        part_copy(g).wait_recv()
        bary_v[:, pl.ds(8 * g, 8), :] = part_v[inp, g] + peer_v[g]

    for piece in (0, 1):
        cot_copy(piece, inp).wait_send()
    for g in range(4):
        part_copy(g).wait_send()
    for side in (0, 1):
        if rx:
            @pl.when(has_x[side])
            def _(side=side):
                for turn in range(3):
                    for g in range(4):
                        x_copy(turn, g, side).wait_send()
        if ry:
            @pl.when(has_y[side])
            def _(side=side):
                for turn in range(3):
                    y_copy(turn, side).wait_send()


def fused(rx, ry, weights, warm, log_inputs, cotangent):
    hx = BLOCK * rx
    hbm = pl.BlockSpec(memory_space=pltpu.HBM)
    smem = pl.BlockSpec(memory_space=pltpu.SMEM)
    vmem = pl.BlockSpec(memory_space=pltpu.VMEM)
    dma = pltpu.SemaphoreType.DMA
    field = pltpu.VMEM((16, 32, 256), F32)
    halves = pltpu.VMEM((2, 16, 32, 128), F32)
    rows_y = 16 if ry == 2 else 8
    matrix = pltpu.VMEM((256, 256), BF16)
    return pl.pallas_call(
        functools.partial(kernel, rx, ry),
        out_shape=(
            jax.ShapeDtypeStruct((16, 32, 128), F32),
            jax.ShapeDtypeStruct((16, 32, 256), F32),
        ),
        in_specs=[smem, hbm, hbm, hbm],
        out_specs=(vmem, vmem),
        scratch_shapes=[
            field, field, halves,
            pltpu.VMEM((6, 4, 16, 8, 256), F32),
            pltpu.VMEM((4, 16, 8, 256), F32),
            pltpu.VMEM((3, 4, 2, max(hx, 1), 8, 256), F32),
            pltpu.VMEM((3, 2, rows_y, 8, 256), F32),
            pltpu.VMEM((3, 2, rows_y, 8, 256), F32),
            pltpu.VMEM((4, 128, 256), F32),
            pltpu.VMEM((4, 128, 256), F32),
            pltpu.VMEM((4, 128, 256), BF16),
            pltpu.VMEM((4, 128, 256), BF16),
            pltpu.VMEM((2, 4, 16, 8, 128), F32),
            pltpu.VMEM((4, 16, 8, 128), F32),
            matrix,
            pltpu.VMEM((256, 32 * max(hx, 4)), BF16),
            matrix,
            pltpu.VMEM((512 if ry == 1 else 256, 256), BF16),
            matrix, matrix,
            dma((3,)), dma((3, 4, 2)), dma((3, 4, 2)), dma((3, 2)), dma((3, 2)), dma((6,)), dma((6,)),
        ],
        compiler_params=pltpu.CompilerParams(
            collective_id=3 * rx + ry, has_side_effects=True, vmem_limit_bytes=40 << 20
        ),
    )(weights, warm, log_inputs, cotangent)


def store(bary_v, grad_v, bary_hbm, grad_hbm, sems):
    copies = [
        pltpu.make_async_copy(bary_v, bary_hbm, sems.at[0]),
        pltpu.make_async_copy(grad_v, grad_hbm, sems.at[1]),
    ]
    for copy in copies:
        copy.start()
    for copy in copies:
        copy.wait()


def stored(bary, grad):
    vmem = pl.BlockSpec(memory_space=pltpu.VMEM)
    hbm = pl.BlockSpec(memory_space=pltpu.HBM)
    return pl.pallas_call(
        store,
        out_shape=(
            jax.ShapeDtypeStruct(bary.shape, F32),
            jax.ShapeDtypeStruct(grad.shape, F32),
        ),
        in_specs=[vmem, vmem],
        out_specs=(hbm, hbm),
        scratch_shapes=[pltpu.SemaphoreType.DMA((2,))],
    )(bary, grad)


def choose(reach_ref, index_ref):
    index_ref[0] = 2 * reach_ref[0] + (reach_ref[1] > reach_ref[2]).astype(jnp.int32)


def per_device(log_inputs, warm_potential, bary_weights, band_reach, bary_cotangent):
    index = pl.pallas_call(
        choose,
        out_shape=jax.ShapeDtypeStruct((1,), jnp.int32),
        in_specs=[pl.BlockSpec(memory_space=pltpu.SMEM)],
        out_specs=pl.BlockSpec(memory_space=pltpu.SMEM),
    )(band_reach)[0]
    branches = [functools.partial(fused, rx, ry) for rx, ry in CASES]
    bary, grad = lax.switch(
        index, branches, bary_weights, warm_potential[0], log_inputs[0], bary_cotangent
    )
    bary, grad = stored(bary, grad)
    return bary, grad[None]


def solution(mesh):
    return jax.shard_map(
        per_device,
        mesh=mesh,
        in_specs=(
            P("inp", "pa", "pb", None),
            P("inp", "pa", "pb", None),
            P("inp"),
            P(),
            P("pa", "pb", "inp"),
        ),
        out_specs=(P("pa", "pb", "inp"), P("inp", "pa", "pb", None)),
        check_vma=False,
    )
```

```python
import functools
import math

import jax
import jax.numpy as jnp
from jax import lax
from jax.experimental import pallas as pl
from jax.experimental.pallas import tpu as pltpu
from jax.sharding import PartitionSpec as P

MESH = pl.DeviceIdType.MESH
F32 = jnp.float32
BF16 = jnp.bfloat16
BLOCK = 4
SIGMA = 3.0
OUTER, INNER = (0, 3), (1, 2)
LOG = 4
CASES = ((0, 1), (0, 2), (1, 0), (1, 2), (2, 0), (2, 1))


def weight(row, column, reach):
    offset = (row - column).astype(F32)
    inside = jnp.abs(row // BLOCK - column // BLOCK) <= reach
    gauss = jnp.exp(-offset * offset / (2.0 * SIGMA * SIGMA)) / (SIGMA * math.sqrt(2.0 * math.pi))
    return 0.5 * jnp.where(row == column, 1.0, 0.0) + 0.5 * jnp.where(inside, gauss, 0.0)


def iotas(rows, columns):
    shape = (rows, columns)
    return lax.broadcasted_iota(jnp.int32, shape, 0), lax.broadcasted_iota(jnp.int32, shape, 1)


def split(value):
    high = value.astype(BF16)
    return high, (value - high.astype(F32)).astype(BF16)


def stacked(value):
    return jnp.concatenate(split(value), axis=0)


def doubled(matrix):
    high, low = split(matrix)
    return jnp.concatenate(
        [jnp.concatenate([high, high], axis=1), jnp.concatenate([low, low], axis=1)], axis=0
    )


def dot(a, b):
    return jnp.dot(a, b, preferred_element_type=F32)


def product(left, parts):
    both = dot(left, parts)
    rows = both.shape[0] // 2
    return both[:rows] + both[rows:]


def kernel(
    rx, ry, w_ref, warm_hbm, log_hbm, cot_hbm, bary_v, grad_v,
    warm_v, log_v, cot_v, own, image, x_halo, y_out, y_halo, acc_x, acc_y, v_high, v_low,
    part_v, peer_v, mx, mxh, my, myh, kzh, kzl,
    in_sem, x_send, x_recv, y_send, y_recv, i_send, i_recv,
):
    rz = 3 - rx - ry
    hx = BLOCK * rx
    inp, pa, pb = (lax.axis_index(name) for name in ("inp", "pa", "pb"))
    near_x = ({"pa": pa - 1}, {"pa": pa + 1})
    near_y = ({"pb": pb - 1}, {"pb": pb + 1})
    has_x = (pa > 0, pa < lax.axis_size("pa") - 1)
    has_y = (pb > 0, pb < lax.axis_size("pb") - 1)
    partner = {"inp": 1 - inp}

    loads = [
        pltpu.make_async_copy(warm_hbm, warm_v, in_sem.at[0]),
        pltpu.make_async_copy(cot_hbm, cot_v.at[inp], in_sem.at[1]),
        pltpu.make_async_copy(log_hbm, log_v, in_sem.at[2]),
    ]
    for load in loads:
        load.start()

    barrier = pltpu.get_barrier_semaphore()
    pl.semaphore_signal(barrier, inc=1, device_id=partner, device_id_type=MESH)
    others = 1
    for near, has, used in ((near_x, has_x, rx), (near_y, has_y, ry)):
        for side in (0, 1):
            if used:
                @pl.when(has[side])
                def _(device=near[side]):
                    pl.semaphore_signal(barrier, inc=1, device_id=device, device_id_type=MESH)
                others = others + has[side].astype(jnp.int32)

    for side in (0, 1):
        if rx:
            @pl.when(jnp.logical_not(has_x[side]))
            def _(side=side):
                x_halo[:, :, side] = jnp.zeros((3, 4, hx, 8, 256), F32)
        if ry:
            @pl.when(jnp.logical_not(has_y[side]))
            def _(side=side):
                y_halo[:, side] = jnp.zeros((3, *y_halo.shape[2:]), F32)

    if rx:
        row, column = iotas(128, 128)
        lines = weight(row % 8, column % 8, 0) if ry == 0 else (row % 8 == column % 8).astype(F32)
        mx[...] = doubled(lines * weight(row // 8, column // 8, rx))
        row, column = iotas(128, 16 * hx)
        place = jnp.where(column < 8 * hx, column // 8, 16 + column // 8)
        lines = weight(row % 8, column % 8, 0) if ry == 0 else (row % 8 == column % 8).astype(F32)
        mxh[...] = doubled(lines * weight(row // 8 + hx, place, rx))
    if ry:
        def lines_x(row, column):
            return (row == column).astype(F32) if rx else weight(row, column, 0)

        row, column = iotas(128, 128)
        entries = weight(8 * (row // 32) + row % 8, 8 * (column // 32) + column % 8, ry)
        my[...] = doubled(lines_x((row % 32) // 8, (column % 32) // 8) * entries)
    if ry == 2:
        place = jnp.where(column < 64, column % 8, 40 + column % 8)
        entries = weight(8 + 24 * (row // 64) + row % 8, place, ry)
        myh[...] = doubled(lines_x((row % 64) // 8, (column % 64) // 8) * entries)
    if ry == 1:
        row, column = iotas(256, 128)
        place = jnp.where(column < 64, column % 4, 36 + column % 4)
        entries = weight(4 + 24 * (row // 128) + row % 8, place, ry)
        line = 2 * ((column % 64) // 8) + (column % 8) // 4
        myh[...] = doubled(lines_x((row % 128) // 8, line) * entries)
    row, column = iotas(256, 256)
    kzh[...], kzl[...] = split(weight(row, column, rz))

    def tile(ref, g):
        return ref[:, pl.ds(8 * g, 8), :]

    def remote(source, target, send, recv, device):
        return pltpu.make_async_remote_copy(
            src_ref=source, dst_ref=target, send_sem=send, recv_sem=recv,
            device_id=device, device_id_type=MESH,
        )

    def x_copy(turn, g, side):
        return remote(
            own.at[turn, g, pl.ds(0 if side == 0 else 16 - hx, hx)], x_halo.at[turn, g, 1 - side],
            x_send.at[turn, g, side], x_recv.at[turn, g, 1 - side], near_x[side],
        )

    y_lines = [pl.ds(4, 8), pl.ds(0, 4), pl.ds(12, 4)] if (rx, ry) == (1, 2) else [pl.ds(0, y_out.shape[2])]

    def y_copy(turn, side, piece):
        lines = y_lines[piece]
        source = own.at[turn, OUTER[side], lines] if ry == 2 and rx == 0 else y_out.at[turn, side, lines]
        return remote(
            source, y_halo.at[turn, 1 - side, lines],
            y_send.at[turn, side, piece], y_recv.at[turn, 1 - side, piece], near_y[side],
        )

    def cot_copy(piece, slot):
        rows = pl.ds(8 * piece, 8)
        return remote(
            cot_v.at[slot, rows], cot_v.at[slot, rows], i_send.at[piece], i_recv.at[piece], partner
        )

    def part_copy(g):
        return remote(
            part_v.at[1 - inp, g], peer_v.at[g], i_send.at[2 + g], i_recv.at[2 + g], partner
        )

    def x_start(turn, pair):
        for side in (0, 1):
            @pl.when(has_x[side])
            def _(side=side):
                for g in pair:
                    x_copy(turn, g, side).start()

    def y_start(turn, g, value):
        side = OUTER.index(g)
        if ry == 2 and rx:
            for lines in y_lines[1:]:
                y_out[turn, side, lines] = value[lines.start : lines.start + lines.size]
        if ry == 1:
            value = value.reshape(8, 2, 8, 256)
            start = 4 * side
            y_out[turn, side] = jnp.concatenate(
                [value[:, 0, start : start + 4], value[:, 1, start : start + 4]], axis=1
            )

        @pl.when(has_y[side])
        def _():
            for piece in range(len(y_lines))[-2:]:
                y_copy(turn, side, piece).start()

    def enter(turn, pair):
        if rx:
            x_start(turn, pair)
        else:
            for g in pair:
                if g in OUTER:
                    y_start(turn, g, own[turn, g])

    def own_part(turn, pair):
        for g in pair:
            value = own[turn, g].reshape(128, 256)
            if rx:
                value = product(mx[...], stacked(value))
                acc_x[g] = value
                if ry == 2 and g in OUTER:
                    side = OUTER.index(g)
                    y_out[turn, side, pl.ds(4, 8)] = value.reshape(16, 8, 256)[4:12]

                    @pl.when(has_y[side])
                    def _(side=side):
                        y_copy(turn, side, 0).start()
            else:
                v_high[g], v_low[g] = split(value)

    def x_finish(turn, pair):
        for side in (0, 1):
            @pl.when(has_x[side])
            def _(side=side):
                for g in pair:
                    x_copy(turn, g, 1 - side).wait_recv()
        totals = []
        for g in pair:
            halo = x_halo[turn, g].reshape(16 * hx, 256)
            totals.append(acc_x[g] + product(mxh[...], stacked(halo)))
        return totals

    def y_own():
        for q in range(4):
            rows = pl.ds(32 * q, 32)
            parts = jnp.concatenate(
                [v_high[:, rows].reshape(128, 256), v_low[:, rows].reshape(128, 256)], axis=0
            )
            acc_y[:, rows] = product(my[...], parts).reshape(4, 32, 256)

    def y_finish(turn):
        for side in (0, 1):
            @pl.when(has_y[side])
            def _(side=side):
                for piece in range(len(y_lines)):
                    y_copy(turn, 1 - side, piece).wait_recv()
        if ry == 2:
            pieces = []
            for half in (0, 1):
                halo = y_halo[turn, :, pl.ds(8 * half, 8)].reshape(128, 256)
                pieces.append(product(myh[...], stacked(halo)))
            more = [jnp.concatenate([p[64 * e : 64 * e + 64] for p in pieces], axis=0) for e in (0, 1)]
        else:
            both = product(myh[...], stacked(y_halo[turn].reshape(128, 256)))
            more = [both[:128], both[128:]]
        return [acc_y[g] + extra for g, extra in zip(OUTER, more)]

    def epilogue(turn, pair, totals):
        high, low = split(jnp.concatenate(totals, axis=0))
        both = dot(jnp.concatenate([high, low], axis=0), kzh[...])
        both = both[:256] + both[256:] + dot(high, kzl[...])
        for g, value in zip(pair, (both[:128], both[128:])):
            image[g] = value.reshape(16, 8, 256)

        def part():
            for g in pair:
                value = w_ref[0] * (tile(warm_v, g) + jnp.log(image[g]))
                part_v[0, g] = value[:, :, :128]
                part_v[1, g] = value[:, :, 128:]

        if rx == 0:
            @pl.when(turn == 1)
            def _():
                part()
                for g in pair:
                    part_copy(g).start()

        if pair == first:
            @pl.when(turn == 1)
            def _():
                for piece in (0, 1):
                    cot_copy(piece, 1 - inp).wait_recv()
                for g in range(4):
                    own[LOG + 1, g, :, :, :128] = w_ref[0] * tile(cot_v.at[0], g)
                    own[LOG + 1, g, :, :, 128:] = w_ref[0] * tile(cot_v.at[1], g)

        factor = jnp.where(turn == 2, 1, turn + LOG)
        for g in pair:
            value = image[g]
            own[turn + 1, g] = own[factor, g] * jnp.where(turn == 2, value, 1.0 / value)

        @pl.when(turn < 2)
        def _():
            enter(turn + 1, pair)

        if rx:
            @pl.when(turn == 1)
            def _():
                part()

        @pl.when(turn < 2)
        def _():
            own_part(turn + 1, pair)

    loads[0].wait()
    for g in OUTER + INNER:
        own[0, g] = jnp.exp(tile(warm_v, g))
    loads[1].wait()
    pl.semaphore_wait(barrier, others)

    first, second = (OUTER, INNER) if rx == 2 or ry == 0 else (INNER, OUTER)
    early = (rx, ry) in ((0, 1), (0, 2), (1, 0))

    enter(0, OUTER)
    if rx:
        enter(0, INNER)
    if early:
        cot_copy(0, inp).start()
        cot_copy(1, inp).start()
    own_part(0, OUTER)
    own_part(0, INNER)
    loads[2].wait()
    for g in range(4):
        own[LOG, g] = jnp.exp(tile(log_v, g))

    def body(turn, carry):
        if rx and ry:
            for pair in (OUTER, INNER):
                for g, total in zip(pair, x_finish(turn, pair)):
                    v_high[g], v_low[g] = split(total)
                    if g in OUTER:
                        y_start(turn, g, total.reshape(16, 8, 256))
                if pair == OUTER:
                    @pl.when(turn == 0)
                    def _():
                        cot_copy(0, inp).start()
        if ry:
            y_own()

        for pair in (first, second):
            if ry == 0:
                totals = x_finish(turn, pair)
            elif pair == OUTER:
                totals = y_finish(turn)
            else:
                totals = [acc_y[g] for g in pair]
            epilogue(turn, pair, totals)
            if ry == 0 and not early:
                @pl.when(turn == 0)
                def _(pair=pair):
                    cot_copy((first, second).index(pair), inp).start()

        if rx:
            @pl.when(turn == 1)
            def _():
                for g in first + second:
                    part_copy(g).start()
        if rx and ry:
            @pl.when(turn == 0)
            def _():
                cot_copy(1, inp).start()
        return carry

    lax.fori_loop(0, 3, body, 0)

    for g in range(4):
        grad_v[:, pl.ds(8 * g, 8), :] = own[3, g]
    for g in first + second:
        part_copy(g).wait_recv()
        bary_v[:, pl.ds(8 * g, 8), :] = part_v[inp, g] + peer_v[g]

    for piece in (0, 1):
        cot_copy(piece, inp).wait_send()
    for g in range(4):
        part_copy(g).wait_send()
    for side in (0, 1):
        if rx:
            @pl.when(has_x[side])
            def _(side=side):
                for turn in range(3):
                    for g in range(4):
                        x_copy(turn, g, side).wait_send()
        if ry:
            @pl.when(has_y[side])
            def _(side=side):
                for turn in range(3):
                    for piece in range(len(y_lines)):
                        y_copy(turn, side, piece).wait_send()


def fused(rx, ry, weights, warm, log_inputs, cotangent):
    hx = BLOCK * rx
    hbm = pl.BlockSpec(memory_space=pltpu.HBM)
    smem = pl.BlockSpec(memory_space=pltpu.SMEM)
    vmem = pl.BlockSpec(memory_space=pltpu.VMEM)
    dma = pltpu.SemaphoreType.DMA
    field = pltpu.VMEM((16, 32, 256), F32)
    halves = pltpu.VMEM((2, 16, 32, 128), F32)
    rows_y = 16 if ry == 2 else 8
    matrix = pltpu.VMEM((256, 256), BF16)
    return pl.pallas_call(
        functools.partial(kernel, rx, ry),
        out_shape=(
            jax.ShapeDtypeStruct((16, 32, 128), F32),
            jax.ShapeDtypeStruct((16, 32, 256), F32),
        ),
        in_specs=[smem, hbm, hbm, hbm],
        out_specs=(vmem, vmem),
        scratch_shapes=[
            field, field, halves,
            pltpu.VMEM((6, 4, 16, 8, 256), F32),
            pltpu.VMEM((4, 16, 8, 256), F32),
            pltpu.VMEM((3, 4, 2, max(hx, 1), 8, 256), F32),
            pltpu.VMEM((3, 2, rows_y, 8, 256), F32),
            pltpu.VMEM((3, 2, rows_y, 8, 256), F32),
            pltpu.VMEM((4, 128, 256), F32),
            pltpu.VMEM((4, 128, 256), F32),
            pltpu.VMEM((4, 128, 256), BF16),
            pltpu.VMEM((4, 128, 256), BF16),
            pltpu.VMEM((2, 4, 16, 8, 128), F32),
            pltpu.VMEM((4, 16, 8, 128), F32),
            matrix,
            pltpu.VMEM((256, 32 * max(hx, 4)), BF16),
            matrix,
            pltpu.VMEM((512 if ry == 1 else 256, 256), BF16),
            matrix, matrix,
            dma((3,)), dma((3, 4, 2)), dma((3, 4, 2)), dma((3, 2, 3)), dma((3, 2, 3)), dma((6,)), dma((6,)),
        ],
        compiler_params=pltpu.CompilerParams(
            collective_id=3 * rx + ry, has_side_effects=True, vmem_limit_bytes=40 << 20
        ),
    )(weights, warm, log_inputs, cotangent)


def store(bary_v, grad_v, bary_hbm, grad_hbm, sems):
    copies = [
        pltpu.make_async_copy(bary_v, bary_hbm, sems.at[0]),
        pltpu.make_async_copy(grad_v, grad_hbm, sems.at[1]),
    ]
    for copy in copies:
        copy.start()
    for copy in copies:
        copy.wait()


def stored(bary, grad):
    vmem = pl.BlockSpec(memory_space=pltpu.VMEM)
    hbm = pl.BlockSpec(memory_space=pltpu.HBM)
    return pl.pallas_call(
        store,
        out_shape=(
            jax.ShapeDtypeStruct(bary.shape, F32),
            jax.ShapeDtypeStruct(grad.shape, F32),
        ),
        in_specs=[vmem, vmem],
        out_specs=(hbm, hbm),
        scratch_shapes=[pltpu.SemaphoreType.DMA((2,))],
    )(bary, grad)


def choose(reach_ref, index_ref):
    index_ref[0] = 2 * reach_ref[0] + (reach_ref[1] > reach_ref[2]).astype(jnp.int32)


def per_device(log_inputs, warm_potential, bary_weights, band_reach, bary_cotangent):
    index = pl.pallas_call(
        choose,
        out_shape=jax.ShapeDtypeStruct((1,), jnp.int32),
        in_specs=[pl.BlockSpec(memory_space=pltpu.SMEM)],
        out_specs=pl.BlockSpec(memory_space=pltpu.SMEM),
    )(band_reach)[0]
    branches = [functools.partial(fused, rx, ry) for rx, ry in CASES]
    bary, grad = lax.switch(
        index, branches, bary_weights, warm_potential[0], log_inputs[0], bary_cotangent
    )
    bary, grad = stored(bary, grad)
    return bary, grad[None]


def solution(mesh):
    return jax.shard_map(
        per_device,
        mesh=mesh,
        in_specs=(
            P("inp", "pa", "pb", None),
            P("inp", "pa", "pb", None),
            P("inp"),
            P(),
            P("pa", "pb", "inp"),
        ),
        out_specs=(P("pa", "pb", "inp"), P("inp", "pa", "pb", None)),
        check_vma=False,
    )
```

```python
import functools
import math

import jax
import jax.numpy as jnp
from jax import lax
from jax.experimental import pallas as pl
from jax.experimental.pallas import tpu as pltpu
from jax.sharding import PartitionSpec as P

MESH = pl.DeviceIdType.MESH
F32 = jnp.float32
BF16 = jnp.bfloat16
BLOCK = 4
SIGMA = 3.0
OUTER, INNER = (0, 3), (1, 2)
LOG = 4
CASES = ((0, 1), (0, 2), (1, 0), (1, 2), (2, 0), (2, 1))


def weight(row, column, reach):
    offset = (row - column).astype(F32)
    inside = jnp.abs(row // BLOCK - column // BLOCK) <= reach
    gauss = jnp.exp(-offset * offset / (2.0 * SIGMA * SIGMA)) / (SIGMA * math.sqrt(2.0 * math.pi))
    return 0.5 * jnp.where(row == column, 1.0, 0.0) + 0.5 * jnp.where(inside, gauss, 0.0)


def iotas(rows, columns):
    shape = (rows, columns)
    return lax.broadcasted_iota(jnp.int32, shape, 0), lax.broadcasted_iota(jnp.int32, shape, 1)


def split(value):
    high = value.astype(BF16)
    return high, (value - high.astype(F32)).astype(BF16)


def stacked(value):
    return jnp.concatenate(split(value), axis=0)


def doubled(matrix):
    high, low = split(matrix)
    return jnp.concatenate(
        [jnp.concatenate([high, high], axis=1), jnp.concatenate([low, low], axis=1)], axis=0
    )


def dot(a, b):
    return jnp.dot(a, b, preferred_element_type=F32)


def product(left, parts):
    both = dot(left, parts)
    rows = both.shape[0] // 2
    return both[:rows] + both[rows:]


def kernel(
    rx, ry, w_ref, warm_hbm, log_hbm, cot_hbm, bary_v, grad_v,
    warm_v, log_v, cot_v, own, image, x_halo, y_out, y_halo, acc_x, acc_y, v_high, v_low,
    part_v, peer_v, mx, mxh, my, myh, kzh, kzl,
    in_sem, x_send, x_recv, y_send, y_recv, i_send, i_recv,
):
    rz = 3 - rx - ry
    hx = BLOCK * rx
    inp, pa, pb = (lax.axis_index(name) for name in ("inp", "pa", "pb"))
    near_x = ({"pa": pa - 1}, {"pa": pa + 1})
    near_y = ({"pb": pb - 1}, {"pb": pb + 1})
    has_x = (pa > 0, pa < lax.axis_size("pa") - 1)
    has_y = (pb > 0, pb < lax.axis_size("pb") - 1)
    partner = {"inp": 1 - inp}

    def warm_load(g):
        rows = pl.ds(8 * g, 8)
        return pltpu.make_async_copy(warm_hbm.at[:, rows], warm_v.at[:, rows], in_sem.at[g])

    loads = [
        pltpu.make_async_copy(log_hbm, log_v, in_sem.at[4]),
        pltpu.make_async_copy(cot_hbm, cot_v.at[inp], in_sem.at[5]),
    ]
    for load in [warm_load(g) for g in OUTER + INNER] + loads:
        load.start()

    barrier = pltpu.get_barrier_semaphore()
    pl.semaphore_signal(barrier, inc=1, device_id=partner, device_id_type=MESH)
    others = 1
    for near, has, used in ((near_x, has_x, rx), (near_y, has_y, ry)):
        for side in (0, 1):
            if used:
                @pl.when(has[side])
                def _(device=near[side]):
                    pl.semaphore_signal(barrier, inc=1, device_id=device, device_id_type=MESH)
                others = others + has[side].astype(jnp.int32)

    for side in (0, 1):
        if rx:
            @pl.when(jnp.logical_not(has_x[side]))
            def _(side=side):
                x_halo[:, :, side] = jnp.zeros((3, 4, hx, 8, 256), F32)
        if ry:
            @pl.when(jnp.logical_not(has_y[side]))
            def _(side=side):
                y_halo[:, side] = jnp.zeros((3, *y_halo.shape[2:]), F32)

    def build_matrices():
        if rx:
            row, column = iotas(128, 128)
            lines = weight(row % 8, column % 8, 0) if ry == 0 else (row % 8 == column % 8).astype(F32)
            mx[...] = doubled(lines * weight(row // 8, column // 8, rx))
            row, column = iotas(128, 16 * hx)
            place = jnp.where(column < 8 * hx, column // 8, 16 + column // 8)
            lines = weight(row % 8, column % 8, 0) if ry == 0 else (row % 8 == column % 8).astype(F32)
            mxh[...] = doubled(lines * weight(row // 8 + hx, place, rx))
        if ry:
            def lines_x(row, column):
                return (row == column).astype(F32) if rx else weight(row, column, 0)

            row, column = iotas(128, 128)
            entries = weight(8 * (row // 32) + row % 8, 8 * (column // 32) + column % 8, ry)
            my[...] = doubled(lines_x((row % 32) // 8, (column % 32) // 8) * entries)
        if ry == 2:
            place = jnp.where(column < 64, column % 8, 40 + column % 8)
            entries = weight(8 + 24 * (row // 64) + row % 8, place, ry)
            myh[...] = doubled(lines_x((row % 64) // 8, (column % 64) // 8) * entries)
        if ry == 1:
            row, column = iotas(256, 128)
            place = jnp.where(column < 64, column % 4, 36 + column % 4)
            entries = weight(4 + 24 * (row // 128) + row % 8, place, ry)
            line = 2 * ((column % 64) // 8) + (column % 8) // 4
            myh[...] = doubled(lines_x((row % 128) // 8, line) * entries)
        row, column = iotas(256, 256)
        kzh[...], kzl[...] = split(weight(row, column, rz))

    def tile(ref, g):
        return ref[:, pl.ds(8 * g, 8), :]

    def remote(source, target, send, recv, device):
        return pltpu.make_async_remote_copy(
            src_ref=source, dst_ref=target, send_sem=send, recv_sem=recv,
            device_id=device, device_id_type=MESH,
        )

    def x_copy(turn, g, side):
        return remote(
            own.at[turn, g, pl.ds(0 if side == 0 else 16 - hx, hx)], x_halo.at[turn, g, 1 - side],
            x_send.at[turn, g, side], x_recv.at[turn, g, 1 - side], near_x[side],
        )

    y_lines = [pl.ds(4, 8), pl.ds(0, 4), pl.ds(12, 4)] if (rx, ry) == (1, 2) else [pl.ds(0, y_out.shape[2])]

    def y_copy(turn, side, piece):
        lines = y_lines[piece]
        source = own.at[turn, OUTER[side], lines] if ry == 2 and rx == 0 else y_out.at[turn, side, lines]
        return remote(
            source, y_halo.at[turn, 1 - side, lines],
            y_send.at[turn, side, piece], y_recv.at[turn, 1 - side, piece], near_y[side],
        )

    def cot_copy(piece):
        rows = pl.ds(4 * piece, 4)
        return remote(
            cot_hbm.at[rows], cot_v.at[inp, rows], i_send.at[piece], i_recv.at[piece], partner
        )

    def cot_start(*pieces):
        for piece in pieces:
            cot_copy(piece).start()

    def part_copy(g):
        return remote(
            part_v.at[1 - inp, g], peer_v.at[g], i_send.at[4 + g], i_recv.at[4 + g], partner
        )

    def x_start(turn, pair):
        for side in (0, 1):
            @pl.when(has_x[side])
            def _(side=side):
                for g in pair:
                    x_copy(turn, g, side).start()

    def y_start(turn, g, value):
        side = OUTER.index(g)
        if ry == 2 and rx:
            for lines in y_lines[1:]:
                y_out[turn, side, lines] = value[lines.start : lines.start + lines.size]
        if ry == 1:
            value = value.reshape(8, 2, 8, 256)
            start = 4 * side
            y_out[turn, side] = jnp.concatenate(
                [value[:, 0, start : start + 4], value[:, 1, start : start + 4]], axis=1
            )

        @pl.when(has_y[side])
        def _():
            for piece in range(len(y_lines))[-2:]:
                y_copy(turn, side, piece).start()

    def enter(turn, pair):
        if rx:
            x_start(turn, pair)
        else:
            for g in pair:
                if g in OUTER:
                    y_start(turn, g, own[turn, g])

    def own_part(turn, pair):
        for g in pair:
            value = own[turn, g].reshape(128, 256)
            if rx:
                value = product(mx[...], stacked(value))
                acc_x[g] = value
                if ry == 2 and g in OUTER:
                    side = OUTER.index(g)
                    y_out[turn, side, pl.ds(4, 8)] = value.reshape(16, 8, 256)[4:12]

                    @pl.when(has_y[side])
                    def _(side=side):
                        y_copy(turn, side, 0).start()
            else:
                v_high[g], v_low[g] = split(value)

    def x_finish(turn, pair):
        for side in (0, 1):
            @pl.when(has_x[side])
            def _(side=side):
                for g in pair:
                    x_copy(turn, g, 1 - side).wait_recv()
        totals = []
        for g in pair:
            halo = x_halo[turn, g].reshape(16 * hx, 256)
            totals.append(acc_x[g] + product(mxh[...], stacked(halo)))
        return totals

    def y_own():
        for q in range(4):
            rows = pl.ds(32 * q, 32)
            parts = jnp.concatenate(
                [v_high[:, rows].reshape(128, 256), v_low[:, rows].reshape(128, 256)], axis=0
            )
            acc_y[:, rows] = product(my[...], parts).reshape(4, 32, 256)

    def y_finish(turn):
        for side in (0, 1):
            @pl.when(has_y[side])
            def _(side=side):
                for piece in range(len(y_lines)):
                    y_copy(turn, 1 - side, piece).wait_recv()
        if ry == 2:
            pieces = []
            for half in (0, 1):
                halo = y_halo[turn, :, pl.ds(8 * half, 8)].reshape(128, 256)
                pieces.append(product(myh[...], stacked(halo)))
            more = [jnp.concatenate([p[64 * e : 64 * e + 64] for p in pieces], axis=0) for e in (0, 1)]
        else:
            both = product(myh[...], stacked(y_halo[turn].reshape(128, 256)))
            more = [both[:128], both[128:]]
        return [acc_y[g] + extra for g, extra in zip(OUTER, more)]

    def epilogue(turn, pair, totals):
        high, low = split(jnp.concatenate(totals, axis=0))
        both = dot(jnp.concatenate([high, low], axis=0), kzh[...])
        both = both[:256] + both[256:] + dot(high, kzl[...])
        for g, value in zip(pair, (both[:128], both[128:])):
            image[g] = value.reshape(16, 8, 256)

        def part():
            for g in pair:
                value = w_ref[0] * (tile(warm_v, g) + jnp.log(image[g]))
                part_v[0, g] = value[:, :, :128]
                part_v[1, g] = value[:, :, 128:]

        if rx == 0:
            @pl.when(turn == 1)
            def _():
                part()
                for g in pair:
                    part_copy(g).start()

        if pair == first:
            @pl.when(turn == 1)
            def _():
                for piece in range(4):
                    cot_copy(piece).wait_recv()
                for g in range(4):
                    own[LOG + 1, g, :, :, :128] = w_ref[0] * tile(cot_v.at[0], g)
                    own[LOG + 1, g, :, :, 128:] = w_ref[0] * tile(cot_v.at[1], g)

        factor = jnp.where(turn == 2, 1, turn + LOG)
        for g in pair:
            value = image[g]
            own[turn + 1, g] = own[factor, g] * jnp.where(turn == 2, value, 1.0 / value)

        @pl.when(turn < 2)
        def _():
            enter(turn + 1, pair)

        if rx:
            @pl.when(turn == 1)
            def _():
                part()

        @pl.when(turn < 2)
        def _():
            own_part(turn + 1, pair)

    first, second = (OUTER, INNER) if rx == 2 or ry == 0 else (INNER, OUTER)

    pl.semaphore_wait(barrier, others)
    if rx == 0 or ry == 0:
        cot_start(0, 1)
    for pair in (OUTER, INNER):
        for g in pair:
            warm_load(g).wait()
            own[0, g] = jnp.exp(tile(warm_v, g))
        if rx or pair == OUTER:
            enter(0, pair)
    if rx == 0 or ry == 0:
        cot_start(2, 3)
    build_matrices()
    own_part(0, OUTER)
    own_part(0, INNER)
    for load in loads:
        load.wait()
    for g in range(4):
        own[LOG, g] = jnp.exp(tile(log_v, g))

    def body(turn, carry):
        if rx and ry:
            for pair in (OUTER, INNER):
                for g, total in zip(pair, x_finish(turn, pair)):
                    v_high[g], v_low[g] = split(total)
                    if g in OUTER:
                        y_start(turn, g, total.reshape(16, 8, 256))
                if pair == OUTER:
                    @pl.when(turn == 0)
                    def _():
                        cot_start(0, 1)
        if ry:
            y_own()

        for pair in (first, second):
            if ry == 0:
                totals = x_finish(turn, pair)
            elif pair == OUTER:
                totals = y_finish(turn)
            else:
                totals = [acc_y[g] for g in pair]
            epilogue(turn, pair, totals)

        if rx:
            @pl.when(turn == 1)
            def _():
                for g in first + second:
                    part_copy(g).start()
        if rx and ry:
            @pl.when(turn == 0)
            def _():
                cot_start(2, 3)
        return carry

    lax.fori_loop(0, 3, body, 0)

    for g in range(4):
        grad_v[:, pl.ds(8 * g, 8), :] = own[3, g]
    for g in first + second:
        part_copy(g).wait_recv()
        bary_v[:, pl.ds(8 * g, 8), :] = part_v[inp, g] + peer_v[g]

    for piece in range(4):
        cot_copy(piece).wait_send()
    for g in range(4):
        part_copy(g).wait_send()
    for side in (0, 1):
        if rx:
            @pl.when(has_x[side])
            def _(side=side):
                for turn in range(3):
                    for g in range(4):
                        x_copy(turn, g, side).wait_send()
        if ry:
            @pl.when(has_y[side])
            def _(side=side):
                for turn in range(3):
                    for piece in range(len(y_lines)):
                        y_copy(turn, side, piece).wait_send()


def fused(rx, ry, weights, warm, log_inputs, cotangent):
    hx = BLOCK * rx
    hbm = pl.BlockSpec(memory_space=pltpu.HBM)
    smem = pl.BlockSpec(memory_space=pltpu.SMEM)
    vmem = pl.BlockSpec(memory_space=pltpu.VMEM)
    dma = pltpu.SemaphoreType.DMA
    field = pltpu.VMEM((16, 32, 256), F32)
    halves = pltpu.VMEM((2, 16, 32, 128), F32)
    rows_y = 16 if ry == 2 else 8
    matrix = pltpu.VMEM((256, 256), BF16)
    return pl.pallas_call(
        functools.partial(kernel, rx, ry),
        out_shape=(
            jax.ShapeDtypeStruct((16, 32, 128), F32),
            jax.ShapeDtypeStruct((16, 32, 256), F32),
        ),
        in_specs=[smem, hbm, hbm, hbm],
        out_specs=(vmem, vmem),
        scratch_shapes=[
            field, field, halves,
            pltpu.VMEM((6, 4, 16, 8, 256), F32),
            pltpu.VMEM((4, 16, 8, 256), F32),
            pltpu.VMEM((3, 4, 2, max(hx, 1), 8, 256), F32),
            pltpu.VMEM((3, 2, rows_y, 8, 256), F32),
            pltpu.VMEM((3, 2, rows_y, 8, 256), F32),
            pltpu.VMEM((4, 128, 256), F32),
            pltpu.VMEM((4, 128, 256), F32),
            pltpu.VMEM((4, 128, 256), BF16),
            pltpu.VMEM((4, 128, 256), BF16),
            pltpu.VMEM((2, 4, 16, 8, 128), F32),
            pltpu.VMEM((4, 16, 8, 128), F32),
            matrix,
            pltpu.VMEM((256, 32 * max(hx, 4)), BF16),
            matrix,
            pltpu.VMEM((512 if ry == 1 else 256, 256), BF16),
            matrix, matrix,
            dma((6,)), dma((3, 4, 2)), dma((3, 4, 2)), dma((3, 2, 3)), dma((3, 2, 3)), dma((8,)), dma((8,)),
        ],
        compiler_params=pltpu.CompilerParams(
            collective_id=3 * rx + ry, has_side_effects=True, vmem_limit_bytes=40 << 20
        ),
    )(weights, warm, log_inputs, cotangent)


def store(bary_v, grad_v, bary_hbm, grad_hbm, sems):
    copies = []
    for source, target in ((grad_v, grad_hbm), (bary_v, bary_hbm)):
        for piece in range(4):
            rows = pl.ds(4 * piece, 4)
            sem = sems.at[len(copies)]
            copies.append(pltpu.make_async_copy(source.at[rows], target.at[rows], sem))
    for copy in copies:
        copy.start()
    for copy in copies:
        copy.wait()


def stored(bary, grad):
    vmem = pl.BlockSpec(memory_space=pltpu.VMEM)
    hbm = pl.BlockSpec(memory_space=pltpu.HBM)
    return pl.pallas_call(
        store,
        out_shape=(
            jax.ShapeDtypeStruct(bary.shape, F32),
            jax.ShapeDtypeStruct(grad.shape, F32),
        ),
        in_specs=[vmem, vmem],
        out_specs=(hbm, hbm),
        scratch_shapes=[pltpu.SemaphoreType.DMA((8,))],
    )(bary, grad)


def choose(reach_ref, index_ref):
    index_ref[0] = 2 * reach_ref[0] + (reach_ref[1] > reach_ref[2]).astype(jnp.int32)


def per_device(log_inputs, warm_potential, bary_weights, band_reach, bary_cotangent):
    index = pl.pallas_call(
        choose,
        out_shape=jax.ShapeDtypeStruct((1,), jnp.int32),
        in_specs=[pl.BlockSpec(memory_space=pltpu.SMEM)],
        out_specs=pl.BlockSpec(memory_space=pltpu.SMEM),
    )(band_reach)[0]
    branches = [functools.partial(fused, rx, ry) for rx, ry in CASES]
    bary, grad = lax.switch(
        index, branches, bary_weights, warm_potential[0], log_inputs[0], bary_cotangent
    )
    bary, grad = stored(bary, grad)
    return bary, grad[None]


def solution(mesh):
    return jax.shard_map(
        per_device,
        mesh=mesh,
        in_specs=(
            P("inp", "pa", "pb", None),
            P("inp", "pa", "pb", None),
            P("inp"),
            P(),
            P("pa", "pb", "inp"),
        ),
        out_specs=(P("pa", "pb", "inp"), P("inp", "pa", "pb", None)),
        check_vma=False,
    )
```

```python
import functools
import math

import jax
import jax.numpy as jnp
from jax import lax
from jax.experimental import pallas as pl
from jax.experimental.pallas import tpu as pltpu
from jax.sharding import PartitionSpec as P

MESH = pl.DeviceIdType.MESH
F32 = jnp.float32
BF16 = jnp.bfloat16
BLOCK = 4
SIGMA = 3.0
OUTER, INNER = (0, 3), (1, 2)
LOG = 4
CASES = ((0, 1), (0, 2), (1, 0), (1, 2), (2, 0), (2, 1))


def weight(row, column, reach):
    offset = (row - column).astype(F32)
    inside = jnp.abs(row // BLOCK - column // BLOCK) <= reach
    gauss = jnp.exp(-offset * offset / (2.0 * SIGMA * SIGMA)) / (SIGMA * math.sqrt(2.0 * math.pi))
    return 0.5 * jnp.where(row == column, 1.0, 0.0) + 0.5 * jnp.where(inside, gauss, 0.0)


def iotas(rows, columns):
    shape = (rows, columns)
    return lax.broadcasted_iota(jnp.int32, shape, 0), lax.broadcasted_iota(jnp.int32, shape, 1)


def split(value):
    high = value.astype(BF16)
    return high, (value - high.astype(F32)).astype(BF16)


def stacked(value):
    return jnp.concatenate(split(value), axis=0)


def doubled(matrix):
    high, low = split(matrix)
    return jnp.concatenate(
        [jnp.concatenate([high, high], axis=1), jnp.concatenate([low, low], axis=1)], axis=0
    )


def dot(a, b):
    return jnp.dot(a, b, preferred_element_type=F32)


def product(left, parts):
    both = dot(left, parts)
    rows = both.shape[0] // 2
    return both[:rows] + both[rows:]


def kernel(
    rx, ry, w_ref, warm_hbm, log_hbm, cot_hbm, bary_v, grad_v,
    warm_v, log_v, cot_v, own, image, x_halo, y_out, y_halo, acc_x, acc_y, v_high, v_low,
    part_v, peer_v, mx, mxh, my, myh, kzh, kzl,
    in_sem, x_send, x_recv, y_send, y_recv, i_send, i_recv,
):
    rz = 3 - rx - ry
    hx = BLOCK * rx
    inp, pa, pb = (lax.axis_index(name) for name in ("inp", "pa", "pb"))
    near_x = ({"pa": pa - 1}, {"pa": pa + 1})
    near_y = ({"pb": pb - 1}, {"pb": pb + 1})
    has_x = (pa > 0, pa < lax.axis_size("pa") - 1)
    has_y = (pb > 0, pb < lax.axis_size("pb") - 1)
    partner = {"inp": 1 - inp}

    def warm_load(g):
        rows = pl.ds(8 * g, 8)
        return pltpu.make_async_copy(warm_hbm.at[:, rows], warm_v.at[:, rows], in_sem.at[g])

    loads = [
        pltpu.make_async_copy(log_hbm, log_v, in_sem.at[4]),
        pltpu.make_async_copy(cot_hbm, cot_v.at[inp], in_sem.at[5]),
    ]
    for load in [warm_load(g) for g in OUTER + INNER] + loads:
        load.start()

    barrier = pltpu.get_barrier_semaphore()
    pl.semaphore_signal(barrier, inc=1, device_id=partner, device_id_type=MESH)
    others = 1
    for near, has, used in ((near_x, has_x, rx), (near_y, has_y, ry)):
        for side in (0, 1):
            if used:
                @pl.when(has[side])
                def _(device=near[side]):
                    pl.semaphore_signal(barrier, inc=1, device_id=device, device_id_type=MESH)
                others = others + has[side].astype(jnp.int32)

    for side in (0, 1):
        if rx:
            @pl.when(jnp.logical_not(has_x[side]))
            def _(side=side):
                x_halo[:, :, side] = jnp.zeros((3, 4, hx, 8, 256), F32)
        if ry:
            @pl.when(jnp.logical_not(has_y[side]))
            def _(side=side):
                y_halo[:, side] = jnp.zeros((3, *y_halo.shape[2:]), F32)

    def build_matrices():
        if rx:
            row, column = iotas(128, 128)
            lines = weight(row % 8, column % 8, 0) if ry == 0 else (row % 8 == column % 8).astype(F32)
            mx[...] = doubled(lines * weight(row // 8, column // 8, rx))
            row, column = iotas(128, 16 * hx)
            place = jnp.where(column < 8 * hx, column // 8, 16 + column // 8)
            lines = weight(row % 8, column % 8, 0) if ry == 0 else (row % 8 == column % 8).astype(F32)
            mxh[...] = doubled(lines * weight(row // 8 + hx, place, rx))
        if ry:
            def lines_x(row, column):
                return (row == column).astype(F32) if rx else weight(row, column, 0)

            row, column = iotas(128, 128)
            entries = weight(8 * (row // 32) + row % 8, 8 * (column // 32) + column % 8, ry)
            my[...] = doubled(lines_x((row % 32) // 8, (column % 32) // 8) * entries)
        if ry == 2:
            place = jnp.where(column < 64, column % 8, 40 + column % 8)
            entries = weight(8 + 24 * (row // 64) + row % 8, place, ry)
            myh[...] = doubled(lines_x((row % 64) // 8, (column % 64) // 8) * entries)
        if ry == 1:
            row, column = iotas(256, 128)
            place = jnp.where(column < 64, column % 4, 36 + column % 4)
            entries = weight(4 + 24 * (row // 128) + row % 8, place, ry)
            line = 2 * ((column % 64) // 8) + (column % 8) // 4
            myh[...] = doubled(lines_x((row % 128) // 8, line) * entries)
        row, column = iotas(256, 256)
        kzh[...], kzl[...] = split(weight(row, column, rz))

    def tile(ref, g):
        return ref[:, pl.ds(8 * g, 8), :]

    def remote(source, target, send, recv, device):
        return pltpu.make_async_remote_copy(
            src_ref=source, dst_ref=target, send_sem=send, recv_sem=recv,
            device_id=device, device_id_type=MESH,
        )

    def x_copy(turn, g, side):
        return remote(
            own.at[turn, g, pl.ds(0 if side == 0 else 16 - hx, hx)], x_halo.at[turn, g, 1 - side],
            x_send.at[turn, g, side], x_recv.at[turn, g, 1 - side], near_x[side],
        )

    y_lines = [pl.ds(4, 8), pl.ds(0, 4), pl.ds(12, 4)] if (rx, ry) == (1, 2) else [pl.ds(0, y_out.shape[2])]

    def y_copy(turn, side, piece):
        lines = y_lines[piece]
        source = own.at[turn, OUTER[side], lines] if ry == 2 and rx == 0 else y_out.at[turn, side, lines]
        return remote(
            source, y_halo.at[turn, 1 - side, lines],
            y_send.at[turn, side, piece], y_recv.at[turn, 1 - side, piece], near_y[side],
        )

    def cot_copy(piece):
        rows = pl.ds(4 * piece, 4)
        return remote(
            cot_hbm.at[rows], cot_v.at[inp, rows], i_send.at[piece], i_recv.at[piece], partner
        )

    def cot_start(*pieces):
        for piece in pieces:
            cot_copy(piece).start()

    def part_copy(g):
        return remote(
            part_v.at[1 - inp, g], peer_v.at[g], i_send.at[4 + g], i_recv.at[4 + g], partner
        )

    def x_start(turn, pair):
        for side in (0, 1):
            @pl.when(has_x[side])
            def _(side=side):
                for g in pair:
                    x_copy(turn, g, side).start()

    def y_start(turn, g, value):
        side = OUTER.index(g)
        if ry == 2 and rx:
            for lines in y_lines[1:]:
                y_out[turn, side, lines] = value[lines.start : lines.start + lines.size]
        if ry == 1:
            value = value.reshape(8, 2, 8, 256)
            start = 4 * side
            y_out[turn, side] = jnp.concatenate(
                [value[:, 0, start : start + 4], value[:, 1, start : start + 4]], axis=1
            )

        @pl.when(has_y[side])
        def _():
            for piece in range(len(y_lines))[-2:]:
                y_copy(turn, side, piece).start()

    def enter(turn, pair):
        if rx:
            x_start(turn, pair)
        else:
            for g in pair:
                if g in OUTER:
                    y_start(turn, g, own[turn, g])

    def own_part(turn, pair):
        for g in pair:
            value = own[turn, g].reshape(128, 256)
            if rx:
                value = product(mx[...], stacked(value))
                acc_x[g] = value
                if ry == 2 and g in OUTER:
                    side = OUTER.index(g)
                    y_out[turn, side, pl.ds(4, 8)] = value.reshape(16, 8, 256)[4:12]

                    @pl.when(has_y[side])
                    def _(side=side):
                        y_copy(turn, side, 0).start()
            else:
                v_high[g], v_low[g] = split(value)

    def x_finish(turn, pair):
        for side in (0, 1):
            @pl.when(has_x[side])
            def _(side=side):
                for g in pair:
                    x_copy(turn, g, 1 - side).wait_recv()
        totals = []
        for g in pair:
            halo = x_halo[turn, g].reshape(16 * hx, 256)
            totals.append(acc_x[g] + product(mxh[...], stacked(halo)))
        return totals

    def y_own():
        for q in range(4):
            rows = pl.ds(32 * q, 32)
            parts = jnp.concatenate(
                [v_high[:, rows].reshape(128, 256), v_low[:, rows].reshape(128, 256)], axis=0
            )
            acc_y[:, rows] = product(my[...], parts).reshape(4, 32, 256)

    def y_finish(turn):
        for side in (0, 1):
            @pl.when(has_y[side])
            def _(side=side):
                for piece in range(len(y_lines)):
                    y_copy(turn, 1 - side, piece).wait_recv()
        if ry == 2:
            pieces = []
            for half in (0, 1):
                halo = y_halo[turn, :, pl.ds(8 * half, 8)].reshape(128, 256)
                pieces.append(product(myh[...], stacked(halo)))
            more = [jnp.concatenate([p[64 * e : 64 * e + 64] for p in pieces], axis=0) for e in (0, 1)]
        else:
            both = product(myh[...], stacked(y_halo[turn].reshape(128, 256)))
            more = [both[:128], both[128:]]
        return [acc_y[g] + extra for g, extra in zip(OUTER, more)]

    def epilogue(turn, pair, totals):
        high, low = split(jnp.concatenate(totals, axis=0))
        both = dot(jnp.concatenate([high, low], axis=0), kzh[...])
        both = both[:256] + both[256:] + dot(high, kzl[...])
        for g, value in zip(pair, (both[:128], both[128:])):
            image[g] = value.reshape(16, 8, 256)

        def part():
            for g in pair:
                value = w_ref[0] * (tile(warm_v, g) + jnp.log(image[g]))
                part_v[0, g] = value[:, :, :128]
                part_v[1, g] = value[:, :, 128:]

        if rx == 0:
            @pl.when(turn == 1)
            def _():
                part()
                for g in pair:
                    part_copy(g).start()

        if pair == first:
            @pl.when(turn == 1)
            def _():
                for piece in range(4):
                    cot_copy(piece).wait_recv()
                for g in range(4):
                    own[LOG + 1, g, :, :, :128] = w_ref[0] * tile(cot_v.at[0], g)
                    own[LOG + 1, g, :, :, 128:] = w_ref[0] * tile(cot_v.at[1], g)

        factor = jnp.where(turn == 2, 1, turn + LOG)
        for g in pair:
            value = image[g]
            own[turn + 1, g] = own[factor, g] * jnp.where(turn == 2, value, 1.0 / value)

        @pl.when(turn < 2)
        def _():
            enter(turn + 1, pair)

        if rx:
            @pl.when(turn == 1)
            def _():
                part()
                if ry == 0:
                    for g in pair:
                        part_copy(g).start()

        @pl.when(turn < 2)
        def _():
            own_part(turn + 1, pair)

    first, second = (OUTER, INNER) if rx == 2 or ry == 0 else (INNER, OUTER)

    pl.semaphore_wait(barrier, others)
    if rx == 0 or ry == 0:
        cot_start(0, 1)
    for pair in (OUTER, INNER):
        for g in pair:
            warm_load(g).wait()
            own[0, g] = jnp.exp(tile(warm_v, g))
        if rx or pair == OUTER:
            enter(0, pair)
    if rx == 0 or ry == 0:
        cot_start(2, 3)
    build_matrices()
    own_part(0, OUTER)
    own_part(0, INNER)
    for load in loads:
        load.wait()
    for g in range(4):
        own[LOG, g] = jnp.exp(tile(log_v, g))

    def body(turn, carry):
        if rx and ry:
            for pair in (OUTER, INNER):
                for g, total in zip(pair, x_finish(turn, pair)):
                    v_high[g], v_low[g] = split(total)
                    if g in OUTER:
                        y_start(turn, g, total.reshape(16, 8, 256))
                if pair == OUTER:
                    @pl.when(turn == 0)
                    def _():
                        cot_start(0, 1)
        if ry:
            y_own()

        for pair in (first, second):
            if ry == 0:
                totals = x_finish(turn, pair)
            elif pair == OUTER:
                totals = y_finish(turn)
            else:
                totals = [acc_y[g] for g in pair]
            epilogue(turn, pair, totals)

        if rx and ry:
            @pl.when(turn == 1)
            def _():
                for g in first + second:
                    part_copy(g).start()
        if rx and ry:
            @pl.when(turn == 0)
            def _():
                cot_start(2, 3)
        return carry

    lax.fori_loop(0, 3, body, 0)

    for g in range(4):
        grad_v[:, pl.ds(8 * g, 8), :] = own[3, g]
    for g in first + second:
        part_copy(g).wait_recv()
        bary_v[:, pl.ds(8 * g, 8), :] = part_v[inp, g] + peer_v[g]

    for piece in range(4):
        cot_copy(piece).wait_send()
    for g in range(4):
        part_copy(g).wait_send()
    for side in (0, 1):
        if rx:
            @pl.when(has_x[side])
            def _(side=side):
                for turn in range(3):
                    for g in range(4):
                        x_copy(turn, g, side).wait_send()
        if ry:
            @pl.when(has_y[side])
            def _(side=side):
                for turn in range(3):
                    for piece in range(len(y_lines)):
                        y_copy(turn, side, piece).wait_send()


def fused(rx, ry, weights, warm, log_inputs, cotangent):
    hx = BLOCK * rx
    hbm = pl.BlockSpec(memory_space=pltpu.HBM)
    smem = pl.BlockSpec(memory_space=pltpu.SMEM)
    vmem = pl.BlockSpec(memory_space=pltpu.VMEM)
    dma = pltpu.SemaphoreType.DMA
    field = pltpu.VMEM((16, 32, 256), F32)
    halves = pltpu.VMEM((2, 16, 32, 128), F32)
    rows_y = 16 if ry == 2 else 8
    matrix = pltpu.VMEM((256, 256), BF16)
    return pl.pallas_call(
        functools.partial(kernel, rx, ry),
        out_shape=(
            jax.ShapeDtypeStruct((16, 32, 128), F32),
            jax.ShapeDtypeStruct((16, 32, 256), F32),
        ),
        in_specs=[smem, hbm, hbm, hbm],
        out_specs=(vmem, vmem),
        scratch_shapes=[
            field, field, halves,
            pltpu.VMEM((6, 4, 16, 8, 256), F32),
            pltpu.VMEM((4, 16, 8, 256), F32),
            pltpu.VMEM((3, 4, 2, max(hx, 1), 8, 256), F32),
            pltpu.VMEM((3, 2, rows_y, 8, 256), F32),
            pltpu.VMEM((3, 2, rows_y, 8, 256), F32),
            pltpu.VMEM((4, 128, 256), F32),
            pltpu.VMEM((4, 128, 256), F32),
            pltpu.VMEM((4, 128, 256), BF16),
            pltpu.VMEM((4, 128, 256), BF16),
            pltpu.VMEM((2, 4, 16, 8, 128), F32),
            pltpu.VMEM((4, 16, 8, 128), F32),
            matrix,
            pltpu.VMEM((256, 32 * max(hx, 4)), BF16),
            matrix,
            pltpu.VMEM((512 if ry == 1 else 256, 256), BF16),
            matrix, matrix,
            dma((6,)), dma((3, 4, 2)), dma((3, 4, 2)), dma((3, 2, 3)), dma((3, 2, 3)), dma((8,)), dma((8,)),
        ],
        compiler_params=pltpu.CompilerParams(
            collective_id=3 * rx + ry, has_side_effects=True, vmem_limit_bytes=40 << 20
        ),
    )(weights, warm, log_inputs, cotangent)


def store(bary_v, grad_v, bary_hbm, grad_hbm, sems):
    copies = []
    for source, target in ((grad_v, grad_hbm), (bary_v, bary_hbm)):
        for piece in range(4):
            rows = pl.ds(4 * piece, 4)
            sem = sems.at[len(copies)]
            copies.append(pltpu.make_async_copy(source.at[rows], target.at[rows], sem))
    for copy in copies:
        copy.start()
    for copy in copies:
        copy.wait()


def stored(bary, grad):
    vmem = pl.BlockSpec(memory_space=pltpu.VMEM)
    hbm = pl.BlockSpec(memory_space=pltpu.HBM)
    return pl.pallas_call(
        store,
        out_shape=(
            jax.ShapeDtypeStruct(bary.shape, F32),
            jax.ShapeDtypeStruct(grad.shape, F32),
        ),
        in_specs=[vmem, vmem],
        out_specs=(hbm, hbm),
        scratch_shapes=[pltpu.SemaphoreType.DMA((8,))],
    )(bary, grad)


def choose(reach_ref, index_ref):
    index_ref[0] = 2 * reach_ref[0] + (reach_ref[1] > reach_ref[2]).astype(jnp.int32)


def per_device(log_inputs, warm_potential, bary_weights, band_reach, bary_cotangent):
    index = pl.pallas_call(
        choose,
        out_shape=jax.ShapeDtypeStruct((1,), jnp.int32),
        in_specs=[pl.BlockSpec(memory_space=pltpu.SMEM)],
        out_specs=pl.BlockSpec(memory_space=pltpu.SMEM),
    )(band_reach)[0]
    branches = [functools.partial(fused, rx, ry) for rx, ry in CASES]
    bary, grad = lax.switch(
        index, branches, bary_weights, warm_potential[0], log_inputs[0], bary_cotangent
    )
    bary, grad = stored(bary, grad)
    return bary, grad[None]


def solution(mesh):
    return jax.shard_map(
        per_device,
        mesh=mesh,
        in_specs=(
            P("inp", "pa", "pb", None),
            P("inp", "pa", "pb", None),
            P("inp"),
            P(),
            P("pa", "pb", "inp"),
        ),
        out_specs=(P("pa", "pb", "inp"), P("inp", "pa", "pb", None)),
        check_vma=False,
    )
```
